256 devices in a mesh: comp: 2 (over x_hi), gx: 64 (over z, y, core), gy: 2 (over x_lo).
Axes of the slice: x: 4 (x_hi: 2, x_lo: 2; x = x_hi * 2 + x_lo), y: 4, z: 8, core: 2. Of those that a mesh axis runs over, the one named last changes fastest.
Arguments:
- state: float32 [2, 2, 64, 1024, 256], P('comp', None, None, 'gx', 'gy'), may hold values from -6 to 6
- diffusion: float32 [2, 1024, 256], P('comp', 'gx', 'gy'), may hold values from 0.03 to 0.15
- vertical: float32 [2, 64], P('comp'), may hold values from 0.01 to 0.1
- coupling: float32 [2, 1024, 256], P('comp', 'gx', 'gy'), may hold values from 0.02 to 0.2
- land_sea: int32 [2, 1024, 256], P('comp', 'gx', 'gy'), may hold values 0 or 1
- route_tile: int32 [2, 128, 64, 1], P('comp', ('gx', 'gy')), may hold values from 0 to 127; in each aligned block of 64 rows (0 to 63, 64 to 127, ..., all dimensions but the last counted through in order) at most 2 rows name the same one
- route_src: int32 [2, 128, 64], P('comp', ('gx', 'gy')), may hold values from 0 to 15
- route_dst: int32 [2, 128, 64], P('comp', ('gx', 'gy')), may hold values from 0 to 15
- pair_cols: int32 [2, 128, 64], P('comp', ('gx', 'gy')), may hold values from 64 to 128
- intersection: bfloat16 [2, 128, 64, 128, 128], P('comp', ('gx', 'gy')), may hold values from 0 to 0.03125
Outputs:
- final_state: float32 [2, 2, 64, 1024, 256], P('comp', None, None, 'gx', 'gy')
The draws below stay inside these ranges and needn't reach their ends.
Inputs may be any that keep to these rules, and one draw needn't show every extreme that they name: `route_tile`: within the 64 pairs of one component's tile no destination tile is named more than 2 times.
All inputs are finite; a program needn't handle non-finite values. No bound on the sum of `land_sea` on one device may be relied on, other than what follows from the above.
Results may differ from the reference program's by a relative error of at most 0.0003.
Values sent between devices are 32-bit elements; how exact they have to be, the bound alone decides.
No kernel may reach another device: no remote copies, remote signals or barrier semaphores. Data moves between devices by JAX's collectives and lax.ppermute only.
A program may use at most 128 MiB of HBM per device.

```python
import math
import jax
import jax.numpy as jnp
import numpy as np
from jax import lax

LEV = 64
KF = 2
BLK = 128
CX = 16
CY = 128
SUBSTEPS = 3
INTERVALS = 2
NX = 1024
NY = 256
NT = 128
NB = 16
P_SIZE = 64
SLOTS = 2
N_GX = 64
N_GY = 2


def set_ends(array, key, smallest, high):
    place = [jax.random.randint(jax.random.fold_in(key, axis), (), 0, length) for axis, length in enumerate(array.shape)]
    longest = array.shape.index(max(array.shape))
    neighbour = place[:longest] + [(place[longest] + 1) % array.shape[longest]] + place[longest + 1:]
    return array.at[tuple(place)].set(smallest).at[tuple(neighbour)].set(high)


def shard_levels(key, extent, cuts, smallest, high):
    def one(dim, parts):
        draws = jax.random.uniform(jax.random.fold_in(jax.random.fold_in(key, 6), dim), (parts,), jnp.float32, smallest / len(cuts), high / len(cuts))
        return jnp.repeat(jnp.exp(draws), extent[dim] // parts).reshape((-1,) + (1,) * (len(extent) - dim - 1))

    gain = one(*cuts[0])
    for cut in cuts[1:]:
        gain = gain * one(*cut)
    return gain


def deal_out(key, own, number, rows, count, top, most, slope):
    ranking = jax.random.permutation(key, count)
    crowded, ordinary = shares(count, rows * top, most, slope, True), shares(count, rows * top, most, slope, False)
    places = jnp.arange(count)

    def named(sizes, rotation):
        used = int((sizes > 0).sum())
        fixed = max(1, used // 4)
        moved = fixed + (places - fixed + rotation * (used - fixed)) % max(1, count - fixed)
        return jnp.zeros((count,), jnp.int32).at[ranking[jnp.where(places < fixed, places, moved)]].set(jnp.asarray(sizes, jnp.int32))

    sizes = jnp.where(number % 4 == 0, named(crowded, number // 4), named(ordinary, number - number // 4 - 1))
    mixed = jax.random.permutation(jax.random.fold_in(own, 3), count)
    giver, taker = mixed[0:count // 2 * 2:2], mixed[1:count // 2 * 2:2]
    margin = jnp.minimum(sizes[giver] - 1, most - sizes[taker]) // 2
    margin = jnp.where((giver == ranking[0]) | (taker == ranking[0]) | (sizes[taker] == 0), 0, jnp.maximum(margin, 0))
    moved = jax.random.randint(jax.random.fold_in(own, 4), (count // 2,), 0, 1 << 20) % (margin + 1)
    sizes = sizes.at[giver].add(-moved).at[taker].add(moved)
    items = jnp.searchsorted(jnp.cumsum(sizes), jnp.arange(rows * top), side="right").astype(jnp.int32)
    listing = items.reshape(top, rows).T
    listing = listing[jax.random.permutation(jax.random.fold_in(own, 1), rows)]
    rotation = jax.random.randint(jax.random.fold_in(own, 2), (rows, 1), 0, top)
    return jnp.take_along_axis(listing, (jnp.arange(top)[None, :] + rotation) % top, axis=1)


def shares(amount, total, limit, skew, full):
    weights = [(1 << 20) // math.isqrt(grade ** skew) + 1 for grade in range(1, amount + 1)]
    largest = limit if full else min(limit, max(-(-total // amount), total * weights[0] // sum(weights)))
    least = 1 if total - largest >= amount - 1 else 0
    counts, spare = [largest] + [least] * (amount - 1), total - largest - least * (amount - 1)
    while spare > 0:
        free = [i for i in range(1, amount) if counts[i] < largest] or [i for i in range(1, amount) if counts[i] < limit]
        whole, left = sum([weights[i] for i in free]), spare
        for i in free:
            addition = min(limit - counts[i], max(1, left * weights[i] // whole), spare)
            counts[i] = counts[i] + addition
            spare = spare - addition
    return np.array(counts)


def gaussian(rng, shape, width, bound, cuts=(), dtype=jnp.bfloat16):
    loudness = shard_levels(rng, shape, cuts, -0.22, 0.18) if cuts else 1.0
    entries = jax.random.normal(rng, shape, jnp.float32) * width * loudness
    return jnp.minimum(jnp.maximum(entries, -bound), bound).astype(dtype)


def setup_inputs(seed: int = 0) -> dict:
    splits = jax.random.split(jax.random.key(seed), 11)
    state = gaussian(splits[0], (2, KF, LEV, NX, NY), 1.0, 6.0, ((0, 2), (3, 64), (4, 2)), jnp.float32)
    diffusion = jnp.clip(jnp.exp(math.log(0.15) - 1.609438 * jax.random.uniform(splits[1], (2, NX, NY), jnp.float32) ** shard_levels(splits[1], (2, NX, NY), ((0, 2), (1, 64), (2, 2)), -0.2, 0.2)), 0.03, 0.15)
    vertical = jnp.clip(jnp.exp(math.log(0.1) - 2.3025851 * jax.random.uniform(splits[2], (2, LEV), jnp.float32) ** shard_levels(splits[2], (2, LEV), ((0, 2),), -0.2, 0.2)), 0.01, 0.1)
    coupling = jnp.clip(jnp.exp(math.log(0.2) - 2.3025851 * jax.random.uniform(splits[3], (2, NX, NY), jnp.float32) ** shard_levels(splits[3], (2, NX, NY), ((0, 2), (1, 64), (2, 2)), -0.2, 0.2)), 0.02, 0.2)
    land_sea = set_ends((jax.random.randint(splits[4], (2, NX, NY), 0, 10) < 7).astype(jnp.int32), jax.random.fold_in(splits[4], 1), 0, 1)
    route_tile_keys = jax.random.split(jax.random.fold_in(splits[5], 1), 2 * NT * P_SIZE // P_SIZE)
    route_tile_turns = jax.random.permutation(jax.random.fold_in(splits[5], 3), 2 * NT * P_SIZE // P_SIZE)
    route_tile = jax.vmap(lambda own, number: deal_out(jax.random.fold_in(splits[5], 2), own, number, P_SIZE, NT, 1, SLOTS, 2))(route_tile_keys, route_tile_turns).reshape((2, NT, P_SIZE, 1))
    route_src = set_ends(jax.random.randint(splits[6], (2, NT, P_SIZE), 0, NB), jax.random.fold_in(splits[6], 1), 0, NB - 1).astype(jnp.int32)
    route_dst = set_ends(jax.random.randint(splits[7], (2, NT, P_SIZE), 0, NB), jax.random.fold_in(splits[7], 1), 0, NB - 1).astype(jnp.int32)
    pair_cols = set_ends(jax.random.randint(splits[8], (2, NT, P_SIZE), 64, 129), jax.random.fold_in(splits[8], 1), 64, 128).astype(jnp.int32)
    intersection = jnp.clip(0.03125 * jax.random.uniform(splits[9], (2, NT, P_SIZE, BLK, BLK), jnp.float32) ** shard_levels(splits[9], (2, NT, P_SIZE, BLK, BLK), ((0, 2), (1, 128)), -0.2, 0.2), 0.0, 0.03125).astype(jnp.bfloat16)
    return dict(state=state, diffusion=diffusion, vertical=vertical, coupling=coupling, land_sea=land_sea, route_tile=route_tile, route_src=route_src, route_dst=route_dst, pair_cols=pair_cols, intersection=intersection)


def advance(padded, diff_num, mix_num, couple_num, gate, target):
    center = padded[:, :, 1:-1, 1:-1]
    lap_h = padded[:, :, 2:, 1:-1] + padded[:, :, :-2, 1:-1] + padded[:, :, 1:-1, 2:] + padded[:, :, 1:-1, :-2] - 4.0 * center
    column = jnp.concatenate([center[:, :1], center, center[:, -1:]], axis=1)
    lap_v = column[:, 2:] - 2.0 * center + column[:, :-2]
    tend = diff_num[None, None] * lap_h + mix_num[None, :, None, None] * lap_v
    force = couple_num[None] * (target - center[:, 0])
    tend = jnp.concatenate([tend[:, :1] + force[:, None], tend[:, 1:]], axis=1)
    return center + gate[None, None] * tend


def to_tiles(field):
    return field.reshape(KF, N_GX, CX, N_GY, CY).transpose(1, 3, 0, 2, 4).reshape(NT, KF, NB, BLK)


def from_tiles(tiled):
    return tiled.reshape(N_GX, N_GY, KF, CX, CY).transpose(2, 0, 3, 1, 4).reshape(KF, NX, NY)


def remap_one(fields_s, tile_s, src_s, dst_s, cols_s, weights_s):
    surface = fields_s[:, 0].astype(jnp.bfloat16)
    tiled = to_tiles(surface)
    lanes = jnp.arange(BLK)

    def per_tile(packed):
        blocks, sources, weights, cols = packed
        picked = blocks[:, sources].astype(jnp.float32)
        contrib = jnp.einsum('pij,kpj->pki', weights.astype(jnp.float32), picked, precision=lax.Precision.HIGHEST)
        rowmask = (lanes[None, :] < cols[:, None]).astype(jnp.float32)
        return contrib * rowmask[:, None, :]

    contrib = lax.map(per_tile, (tiled, src_s, weights_s, cols_s))
    segment = (tile_s[:, :, 0] * NB + dst_s).reshape(-1)
    summed = jax.ops.segment_sum(contrib.reshape(NT * P_SIZE, KF, BLK), segment, num_segments=NT * NB)
    summed = summed.reshape(NT, NB, KF, BLK).transpose(0, 2, 1, 3)
    return from_tiles(summed)


def reference(state, diffusion, vertical, coupling, land_sea, route_tile, route_src, route_dst, pair_cols, intersection):
    fields = [state[0], state[1]]
    sea = land_sea.astype(jnp.float32)
    gates = [jnp.ones_like(sea[0]), sea[1]]
    for interval in range(INTERVALS):
        sent = [remap_one(fields[s], route_tile[s], route_src[s], route_dst[s], pair_cols[s], intersection[s]) for s in range(2)]
        arrived = [sent[1], sent[0]]
        for s in range(2):
            target = sea[s][None] * arrived[s]
            current = fields[s]
            for sub in range(SUBSTEPS):
                padded = jnp.pad(current, ((0, 0), (0, 0), (1, 1), (1, 1)), mode='wrap')
                current = advance(padded, diffusion[s], vertical[s], coupling[s], gates[s], target)
            fields[s] = current
    return jnp.stack(fields)
```

```python
import jax
import jax.numpy as jnp
from jax import lax
from jax.experimental import pallas as pl
from jax.experimental.pallas import tpu as pltpu
from jax.sharding import PartitionSpec as P

SUBSTEPS = 3
INTERVALS = 2
LANES = 128
CX = 16
WIDE = 144
HALO = 3
CHUNK = 9
AXES = ("comp", "gx", "gy")
VMEM_LIMIT = 48 * 2**20

f32 = jnp.float32


def params(**kw):
    return pltpu.CompilerParams(vmem_limit_bytes=VMEM_LIMIT, **kw)


def lane_ids(rows=1):
    return lax.broadcasted_iota(jnp.int32, (rows, LANES), 1)


def exact_dot(a, b):
    return lax.dot_general(
        a, b, (((1,), (0,)), ((), ())), precision=lax.Precision.HIGHEST, preferred_element_type=f32
    )


def contrib_kernel(tile_ref, src_ref, dst_ref, cols_ref, top_ref, w_ref, send_ref, surf, count):
    step = pl.program_id(0)
    per = w_ref.shape[0]

    @pl.when(step == 0)
    def _():
        send_ref[...] = jnp.zeros_like(send_ref)
        for f in range(2):
            surf[pl.ds(f, CX, stride=8), :] = top_ref[f].astype(jnp.bfloat16).astype(f32)

        def clear(i, c):
            count[i] = 0
            return c

        lax.fori_loop(0, count.shape[0], clear, 0)

    lanes = lane_ids()
    for i in range(per):
        p = step * per + i
        dest = tile_ref[p]
        slot = count[dest]
        count[dest] = slot + 1
        group = dest // 2
        part = dest - 2 * group
        base = group * CHUNK
        picked = surf[pl.ds(pl.multiple_of(src_ref[p] * 8, 8), 8), :].astype(jnp.bfloat16)
        out = lax.dot_general(
            picked, w_ref[i], (((1,), (1,)), ((), ())), preferred_element_type=f32
        )
        out = jnp.where(lanes < cols_ref[p], out, 0.0)
        row = base + part * 4 + slot * 2
        send_ref[pl.ds(row, 1), :] = out[0:1]
        send_ref[pl.ds(row + 1, 1), :] = out[1:2]
        mark = jnp.where(lanes == (part * 2 + slot) * CX + dst_ref[p], 1.0, 0.0)
        send_ref[pl.ds(base + 8, 1), :] += mark


def contributions(top, routes, weights, columns):
    pairs = weights.shape[0]
    per = 16
    tile, src, dst, cols = routes
    smem = pl.BlockSpec(memory_space=pltpu.SMEM)
    return pl.pallas_call(
        contrib_kernel,
        grid=(pairs // per,),
        in_specs=[smem] * 4
        + [
            pl.BlockSpec((2, CX, LANES), lambda i: (0, 0, 0)),
            pl.BlockSpec((per, LANES, LANES), lambda i: (i, 0, 0)),
        ],
        out_specs=pl.BlockSpec((columns * CHUNK, LANES), lambda i: (0, 0)),
        out_shape=jax.ShapeDtypeStruct((columns * CHUNK, LANES), f32),
        scratch_shapes=[pltpu.VMEM((LANES, LANES), f32), pltpu.SMEM((2 * columns,), jnp.int32)],
        compiler_params=params(),
        name="contrib",
    )(tile, src, dst, cols, top, weights)


def write_edges(row_of, low_ref, high_ref, side_ref, clow_ref, chigh_ref):
    sub = lax.broadcasted_iota(jnp.int32, (8, LANES), 0)
    for x in range(CX):
        row = row_of(x)
        side = jnp.where(sub < 4, row[0:8], row[120:128])
        side_ref[pl.ds(x * 8, 8), :] = side
        if x < HALO:
            low_ref[pl.ds(x * LANES, LANES), :] = row
            clow_ref[pl.ds(x * 8, 8), :] = side
        if x >= CX - HALO:
            j = x - (CX - HALO)
            high_ref[pl.ds(j * LANES, LANES), :] = row
            chigh_ref[pl.ds(j * 8, 8), :] = side


def prepare_kernel(
    info_ref, state_ref, diff_ref, coup_ref, sea_ref,
    cells_ref, own_ref, low_ref, high_ref, side_ref, clow_ref, chigh_ref,
):
    sea = sea_ref[...].astype(f32)
    gate = jnp.where(info_ref[0] == 1, sea, jnp.ones_like(sea))
    coup = gate * coup_ref[...]
    own_ref[0:16] = gate * diff_ref[...]
    own_ref[16:32] = gate
    own_ref[32:48] = coup
    own_ref[48:64] = coup * sea
    for x in range(CX):
        cells_ref[x] = state_ref[pl.ds(x, LANES, stride=CX), :].T
    write_edges(lambda x: cells_ref[x], low_ref, high_ref, side_ref, clow_ref, chigh_ref)
    side_ref[128:192] = own_ref[...]
    for k in range(4):
        first = own_ref[pl.ds(k * CX, 2), :]
        last = own_ref[pl.ds(k * CX + CX - 2, 2), :]
        low_ref[pl.ds(HALO * LANES + 2 * k, 2), :] = first
        clow_ref[pl.ds(HALO * 8 + 2 * k, 2), :] = first
        high_ref[pl.ds(HALO * LANES + 2 * k, 2), :] = last
        chigh_ref[pl.ds(HALO * 8 + 2 * k, 2), :] = last


def edge_shapes(with_params):
    more = 8 if with_params else 0
    rows = [HALO * LANES + more] * 2 + [CX * 8 + (64 if with_params else 0)] + [HALO * 8 + more] * 2
    return [jax.ShapeDtypeStruct((r, LANES), f32) for r in rows]


def prepare(info, state, diffusion, coupling, land_sea):
    vmem = pl.BlockSpec(memory_space=pltpu.VMEM)
    return pl.pallas_call(
        prepare_kernel,
        in_specs=[pl.BlockSpec(memory_space=pltpu.SMEM)] + [vmem] * 4,
        out_specs=[vmem] * 7,
        out_shape=[
            jax.ShapeDtypeStruct((CX, LANES, LANES), f32),
            jax.ShapeDtypeStruct((64, LANES), f32),
        ]
        + edge_shapes(True),
        compiler_params=params(),
        name="prepare",
    )(info, state, diffusion, coupling, land_sea)


def densify_kernel(got_ref, dense_ref):
    columns = got_ref.shape[0] // CHUNK
    marks = got_ref[pl.ds(8, columns, stride=CHUNK), :]
    marks = jnp.concatenate([marks, jnp.zeros((LANES - columns, LANES), f32)], axis=0).T
    for part in range(2):
        total = None
        for slot in range(2):
            k = part * 4 + slot * 2
            vals = jnp.concatenate(
                [got_ref[pl.ds(k + f, columns, stride=CHUNK), :] for f in range(2)], axis=1
            )
            vals = jnp.concatenate([vals, jnp.zeros((LANES - columns, 2 * LANES), f32)], axis=0)
            seg = (part * 2 + slot) * CX
            here = exact_dot(marks[seg : seg + CX], vals)
            total = here if total is None else total + here
        for f in range(2):
            dense_ref[pl.ds(part * 2 + f, CX, stride=4), :] = total[:, f * LANES : (f + 1) * LANES]


def densify(got):
    vmem = pl.BlockSpec(memory_space=pltpu.VMEM)
    return pl.pallas_call(
        densify_kernel,
        in_specs=[vmem],
        out_specs=vmem,
        out_shape=jax.ShapeDtypeStruct((64, LANES), f32),
        compiler_params=params(),
        name="densify",
    )(got)


def widen(own, other):
    return jnp.concatenate([other[120:128], own, other[0:8]], axis=0)


def steps_kernel(last, *refs):
    (info_ref, mix_ref, cells_ref, own_ref, plow_ref, phigh_ref, pside_ref, pclow_ref, pchigh_ref) = refs[:9]
    (hlow_ref, hhigh_ref, hside_ref, hclow_ref, hchigh_ref) = refs[9:14]
    (a_ref, b_ref, l1_ref, l2_ref, h1_ref, h2_ref) = refs[14:20]
    if last:
        out_ref = refs[20]
        scratch = refs[21:]
    else:
        out_ref, top_ref, elow_ref, ehigh_ref, eside_ref, eclow_ref, echigh_ref = refs[20:27]
        scratch = refs[27:]
    fa, fb, diff, gate, force, damp, work = scratch
    north = info_ref[1] == 1
    lanes = lane_ids()
    level = jnp.where(lanes >= 64, lanes - 64, lanes)
    mix = mix_ref[...]
    mix_up = jnp.where(level == 63, 0.0, mix)
    mix_low = jnp.where(level == 0, 0.0, mix)
    mix_mid = -(mix_up + mix_low)

    fa[3:19, 8:136] = cells_ref[...]
    for j in range(HALO):
        fa[j, 8:136] = hhigh_ref[pl.ds(j * LANES, LANES), :]
        fa[19 + j, 8:136] = hlow_ref[pl.ds(j * LANES, LANES), :]
        for at in (0, 136):
            fa[j, at : at + 8] = hchigh_ref[pl.ds(j * 8, 8), :]
            fa[19 + j, at : at + 8] = hclow_ref[pl.ds(j * 8, 8), :]
    for x in range(CX):
        for at in (0, 136):
            fa[3 + x, at : at + 8] = hside_ref[pl.ds(x * 8, 8), :]

    def natural(k, part):
        if part == 0:
            low, mid, high = plow_ref, own_ref, phigh_ref
            lo = high[pl.ds(HALO * LANES + 2 * k, 2), :]
            hi = low[pl.ds(HALO * LANES + 2 * k, 2), :]
            return lo, mid[pl.ds(k * CX, CX), :], hi
        lo = pchigh_ref[pl.ds(HALO * 8 + 2 * k, 2), :]
        hi = pclow_ref[pl.ds(HALO * 8 + 2 * k, 2), :]
        return lo, pside_ref[pl.ds(128 + k * CX, CX), :], hi

    def arrived(f, part):
        def pick(even, odd):
            return jnp.where(north, odd, even) if part == 0 else jnp.where(north, even, odd)

        mid = pick(
            a_ref[pl.ds(f, CX, stride=4), :] + b_ref[pl.ds(f, CX, stride=4), :],
            a_ref[pl.ds(2 + f, CX, stride=4), :] + b_ref[pl.ds(2 + f, CX, stride=4), :],
        )

        def edge(u, v):
            return pick(
                u[pl.ds(f, 2, stride=4), :] + v[pl.ds(f, 2, stride=4), :],
                u[pl.ds(2 + f, 2, stride=4), :] + v[pl.ds(2 + f, 2, stride=4), :],
            )

        return edge(l1_ref, l2_ref), mid, edge(h1_ref, h2_ref)

    work[...] = jnp.zeros_like(work)

    def columns_of(first, second):
        wide = []
        for part in range(2):
            for half, make in enumerate((first, second)):
                lo, mid, hi = make(part)
                work[pl.ds(half * 64, 2), :] = lo
                work[pl.ds(half * 64 + 2, CX), :] = mid
                work[pl.ds(half * 64 + 18, 2), :] = hi
            wide.append(work[...].T)
        return widen(*wide)

    def forcing(f):
        def make(part):
            return tuple(u * v for u, v in zip(natural(3, part), arrived(f, part)))

        return make

    both = columns_of(lambda part: natural(0, part), lambda part: natural(1, part))
    damping = columns_of(lambda part: natural(2, part), lambda part: natural(2, part))
    forced = columns_of(forcing(0), forcing(1))
    at_top = level == 0
    for x in range(CX + 4):
        diff[x] = jnp.broadcast_to(both[:, x : x + 1], (WIDE, LANES))
        gate[x] = jnp.broadcast_to(both[:, 64 + x : 65 + x], (WIDE, LANES))
        shift = (LANES - x) % LANES
        damp[x] = jnp.where(at_top, pltpu.roll(damping, shift, 1), 0.0)
        force[x] = jnp.where(at_top, pltpu.roll(forced, shift, 1), 0.0)

    def row(src, x):
        c = src[x]
        lap = src[x - 1] + src[x + 1] + pltpu.roll(c, 1, 0) + pltpu.roll(c, WIDE - 1, 0) - 4.0 * c
        vert = mix_up * pltpu.roll(c, LANES - 1, 1) + mix_low * pltpu.roll(c, 1, 1) + mix_mid * c
        return c + (diff[x - 1] * lap + gate[x - 1] * vert + (force[x - 1] - damp[x - 1] * c))

    def first(x, carry):
        fb[x] = row(fa, x)
        return carry

    def second(x, carry):
        fa[x] = row(fb, x)
        return carry

    lax.fori_loop(1, 21, first, 0)
    lax.fori_loop(2, 20, second, 0)
    if last:

        def third(x, carry):
            fb[x] = row(fa, x)
            return carry

        lax.fori_loop(3, 19, third, 0)
        for x in range(CX):
            out_ref[pl.ds(x, LANES, stride=CX), :] = fb[3 + x, 8:136].T
    else:

        def third(x, top):
            new = row(fa, x)[8:136]
            out_ref[x - 3] = new
            return top + pltpu.roll(jnp.where(at_top, new, 0.0), x - 3, 1)

        top = lax.fori_loop(3, 19, third, jnp.zeros((LANES, LANES), f32)).T
        for f in range(2):
            top_ref[f] = top[64 * f : 64 * f + CX]
        write_edges(lambda x: out_ref[x], elow_ref, ehigh_ref, eside_ref, eclow_ref, echigh_ref)


def run_steps(last, info, mix, cells, own, halo_params, halo, hops):
    vmem = pl.BlockSpec(memory_space=pltpu.VMEM)
    if last:
        outs = [jax.ShapeDtypeStruct((2 * 64 * CX, LANES), f32)]
    else:
        outs = [
            jax.ShapeDtypeStruct((CX, LANES, LANES), f32),
            jax.ShapeDtypeStruct((2, CX, LANES), f32),
        ] + edge_shapes(False)
    big = pltpu.VMEM((CX + 6, WIDE, LANES), f32)
    coef = pltpu.VMEM((CX + 4, WIDE, LANES), f32)
    return pl.pallas_call(
        lambda *refs: steps_kernel(last, *refs),
        in_specs=[pl.BlockSpec(memory_space=pltpu.SMEM)] + [vmem] * 19,
        out_specs=[vmem] * len(outs),
        out_shape=outs,
        scratch_shapes=[big, big, coef, coef, coef, coef, pltpu.VMEM((LANES, LANES), f32)],
        compiler_params=params(),
        name="steps",
    )(info, mix, cells, own, *halo_params, *halo, *hops)


def solution(mesh):
    sizes = [mesh.shape[a] for a in AXES]
    comps, columns, halves = sizes

    def sent(value, where):
        pairs = []
        for s in range(comps):
            for g in range(columns):
                for h in range(halves):
                    a, b, c = where(s, g, h)
                    b, c = b % columns, c % halves
                    pairs.append(((s * columns + g) * halves + h, (a * columns + b) * halves + c))
        return lax.ppermute(value, AXES, pairs)

    def exchanged(low, high, side, clow, chigh):
        return (
            sent(low, lambda s, g, h: (s, g - 1, h)),
            sent(high, lambda s, g, h: (s, g + 1, h)),
            sent(side, lambda s, g, h: (s, g, h + 1)),
            sent(clow, lambda s, g, h: (s, g - 1, h + 1)),
            sent(chigh, lambda s, g, h: (s, g + 1, h + 1)),
        )

    def hopped(dense):
        return (
            sent(dense, lambda s, g, h: (1 - s, g, h)),
            sent(dense, lambda s, g, h: (1 - s, g, h + 1)),
            sent(dense[56:], lambda s, g, h: (1 - s, g + 1, h)),
            sent(dense[56:], lambda s, g, h: (1 - s, g + 1, h + 1)),
            sent(dense[:8], lambda s, g, h: (1 - s, g - 1, h)),
            sent(dense[:8], lambda s, g, h: (1 - s, g - 1, h + 1)),
        )

    def body(
        state, diffusion, vertical, coupling, land_sea,
        route_tile, route_src, route_dst, pair_cols, intersection,
    ):
        info = jnp.stack([lax.axis_index("comp"), lax.axis_index("gy")]).astype(jnp.int32)
        mix = jnp.concatenate([vertical, vertical], axis=1)
        routes = (route_tile[0, 0, :, 0], route_src[0, 0], route_dst[0, 0], pair_cols[0, 0])
        weights = intersection[0, 0]
        top = state[0, :, 0]
        cells, own, *edges = prepare(
            info, state.reshape(-1, LANES), diffusion[0], coupling[0], land_sea[0]
        )
        halo_params = halo = None
        for interval in range(INTERVALS):
            send = contributions(top, routes, weights, columns)
            got = lax.all_to_all(send, "gx", 0, 0, tiled=True)
            halo = exchanged(*edges)
            if interval == 0:
                halo_params = halo
            hops = hopped(densify(got))
            last = interval == INTERVALS - 1
            made = run_steps(last, info, mix, cells, own, halo_params, halo, hops)
            if not last:
                cells, top, *edges = made
        return made[0].reshape(state.shape)

    spec = P("comp", "gx", "gy")
    route = P("comp", ("gx", "gy"))
    return jax.shard_map(
        body,
        mesh=mesh,
        in_specs=(
            P("comp", None, None, "gx", "gy"), spec, P("comp", None), spec, spec,
            route, route, route, route, route,
        ),
        out_specs=P("comp", None, None, "gx", "gy"),
        check_vma=False,
    )
```

```python
import jax
import jax.numpy as jnp
from jax import lax
from jax.experimental import pallas as pl
from jax.experimental.pallas import tpu as pltpu
from jax.sharding import PartitionSpec as P

LANES = 128
LEV = 64
CX = 16
WIDE = 144
HALO = 6
CHUNK = 48
NEAR = 8
TALL = CX + 2 * NEAR
RING = 2 * LANES
NAT = 12
AXES = ("comp", "gx", "gy")
VMEM_LIMIT = 48 * 2**20

f32 = jnp.float32
VM = pl.BlockSpec(memory_space=pltpu.VMEM)
SM = pl.BlockSpec(memory_space=pltpu.SMEM)
HB = pl.BlockSpec(memory_space=pltpu.HBM)


def params():
    return pltpu.CompilerParams(vmem_limit_bytes=VMEM_LIMIT)


def struct(*shape):
    return jax.ShapeDtypeStruct(shape, f32)


def in_hbm(*arrays):
    return [pltpu.with_memory_space_constraint(a, pltpu.HBM) for a in arrays]


def exact_dot(a, b):
    return lax.dot_general(
        a, b, (((1,), (0,)), ((), ())), precision=lax.Precision.HIGHEST, preferred_element_type=f32
    )


PARTS = 4


def fetch_start(routes_hbm, routes, w_hbm, w, sems):
    for i in range(4):
        pltpu.make_async_copy(routes_hbm[i], routes[i], sems.at[i]).start()
    per = w.shape[0] // PARTS
    for i in range(PARTS):
        at = pl.ds(i * per, per)
        pltpu.make_async_copy(w_hbm.at[at], w.at[at], sems.at[4 + i]).start()


def write_contributions(routes_hbm, routes, w_hbm, w, sems, surf, count, put, mark):
    tile_ref, src_ref, dst_ref, cols_ref = routes
    for i in range(4):
        pltpu.make_async_copy(routes_hbm[i], routes[i], sems.at[i]).wait()

    def clear(i, c):
        count[i] = 0
        return c

    lax.fori_loop(0, count.shape[0], clear, 0)
    lanes = lax.broadcasted_iota(jnp.int32, (1, LANES), 1)
    per = w.shape[0] // PARTS
    for p in range(w.shape[0]):
        if p % per == 0:
            at = pl.ds(p, per)
            pltpu.make_async_copy(w_hbm.at[at], w.at[at], sems.at[4 + p // per]).wait()
        dest = tile_ref[p]
        slot = count[dest]
        count[dest] = slot + 1
        group = dest // 2
        part = dest - 2 * group
        picked = surf[pl.ds(pl.multiple_of(src_ref[p] * 8, 8), 8), :].astype(jnp.bfloat16)
        out = lax.dot_general(
            picked, w[p], (((1,), (1,)), ((), ())), preferred_element_type=f32
        )
        out = jnp.where(lanes < cols_ref[p], out, 0.0)
        put(group, part * 4 + slot * 2, out)
        if mark is not None:
            hot = (part * 2 + slot) * CX + dst_ref[p]
            mark(group, jnp.where(lanes == hot, 1.0, 0.0))


def pair_scratch(pairs, columns):
    return [pltpu.SMEM((pairs,), jnp.int32)] * 4 + [
        pltpu.VMEM((pairs, LANES, LANES), jnp.bfloat16),
        pltpu.VMEM((LANES, LANES), f32),
        pltpu.SMEM((2 * columns,), jnp.int32),
        pltpu.SemaphoreType.DMA((4 + PARTS,)),
    ]


def rounded(x):
    return x.astype(jnp.bfloat16).astype(f32)


def first_kernel(*refs):
    routes_hbm, w_hbm, state_hbm, send_ref = refs[:4], refs[4], refs[5], refs[6]
    routes, (w, surf, count, sems, top, top_sems) = refs[7:11], refs[11:]
    tops = [
        pltpu.make_async_copy(state_hbm.at[f, 0], top.at[f], top_sems.at[f]) for f in range(2)
    ]
    for copy in tops:
        copy.start()
    fetch_start(routes_hbm, routes, w_hbm, w, sems)
    send_ref[...] = jnp.zeros_like(send_ref)
    for f in range(2):
        tops[f].wait()
        surf[pl.ds(f, CX, stride=8), :] = rounded(top[f])

    def put(group, row, out):
        send_ref[group * 9 + row] = out[0:1]
        send_ref[group * 9 + row + 1] = out[1:2]

    def mark(group, value):
        send_ref[group * 9 + 8] += value

    write_contributions(routes_hbm, routes, w_hbm, w, sems, surf, count, put, mark)


def first_contributions(routes, weights, state, columns):
    pairs = weights.shape[0]
    return pl.pallas_call(
        first_kernel,
        in_specs=[HB] * 6,
        out_specs=VM,
        out_shape=struct(columns * 9, 1, LANES),
        scratch_shapes=pair_scratch(pairs, columns)
        + [pltpu.VMEM((2, CX, LANES), f32), pltpu.SemaphoreType.DMA((2,))],
        compiler_params=params(),
        name="contrib",
    )(*in_hbm(*routes, weights, state))


def prepare_kernel(
    info_ref, state_ref, diff_ref, coup_ref, sea_ref,
    cells_ref, nat_ref, low_ref, high_ref, side_ref, clow_ref, chigh_ref,
):
    sea = sea_ref[...].astype(f32)
    gate = jnp.where(info_ref[0] == 1, sea, jnp.ones_like(sea))
    coup = gate * coup_ref[...]
    nat_ref[0:16] = gate * diff_ref[...]
    nat_ref[16:32] = gate
    nat_ref[32:48] = coup
    nat_ref[48:64] = coup * sea
    for f in range(2):
        nat_ref[64 * (f + 1) : 64 * (f + 2)] = state_ref[f * LEV * CX : f * LEV * CX + 64]
    for x in range(CX):
        row = state_ref[pl.ds(x, LANES, stride=CX), :].T
        cells_ref[x] = row
        for j, piece in enumerate((row[0:8], row[120:128])):
            at = 16 * x + 8 * j
            side_ref[at : at + 8] = piece
            if x < HALO:
                clow_ref[at : at + 8] = piece
            if x >= CX - HALO:
                at -= 16 * (CX - HALO)
                chigh_ref[at : at + 8] = piece
        if x < HALO:
            low_ref[x * LANES : (x + 1) * LANES] = row
        if x >= CX - HALO:
            at = x - (CX - HALO)
            high_ref[at * LANES : (at + 1) * LANES] = row
    side_ref[16 * CX :] = nat_ref[...]
    for k in range(NAT):
        first = nat_ref[k * CX : k * CX + NEAR]
        final = nat_ref[(k + 1) * CX - NEAR : (k + 1) * CX]
        for ref, value, base in (
            (low_ref, first, HALO * LANES),
            (clow_ref, first, HALO * 16),
            (high_ref, final, HALO * LANES),
            (chigh_ref, final, HALO * 16),
        ):
            ref[base + k * NEAR : base + (k + 1) * NEAR] = value


def prepare(info, state, diffusion, coupling, land_sea):
    along = struct(HALO * LANES + NAT * NEAR, LANES)
    corner = struct(HALO * 16 + NAT * NEAR, LANES)
    return pl.pallas_call(
        prepare_kernel,
        in_specs=[SM] + [VM] * 4,
        out_specs=[VM] * 7,
        out_shape=[
            struct(CX, LANES, LANES), struct(NAT * CX, LANES),
            along, along, struct(16 * CX + NAT * CX, LANES), corner, corner,
        ],
        compiler_params=params(),
        name="prepare",
    )(info, state, diffusion, coupling, land_sea)


def linear_step(planes, made, mixing, diff, gate, damp):
    out = []
    for k in range(made):
        c = planes[k] if k < len(planes) else None
        vert = None

        def add(total, term):
            return term if total is None else total + term

        m = mixing[k]
        if k + 1 < len(planes):
            vert = add(vert, m * planes[k + 1])
        if k > 0:
            vert = add(vert, m * planes[k - 1])
        if c is None:
            out.append(gate * vert)
            continue
        vert = add(vert, -(m if k == 0 else 2.0 * m) * c)
        lap = (
            pltpu.roll(c, 1, 0) + pltpu.roll(c, TALL - 1, 0)
            + pltpu.roll(c, 1, 1) + pltpu.roll(c, RING - 1, 1) - 4.0 * c
        )
        new = c + (diff * lap + gate * vert)
        out.append(new - damp * c if k == 0 else new)
    return out


def coefs(coef_ref):
    return [coef_ref[k * TALL : (k + 1) * TALL] for k in range(4)]


def gather_kernel(mix_ref, nat_ref, low_ref, high_ref, side_ref, clow_ref, chigh_ref, coef_ref, top_ref):
    def plane(k):
        own = [high_ref[HALO * LANES + k * NEAR : HALO * LANES + (k + 1) * NEAR],
               nat_ref[k * CX : (k + 1) * CX],
               low_ref[HALO * LANES + k * NEAR : HALO * LANES + (k + 1) * NEAR]]
        other = [chigh_ref[HALO * 16 + k * NEAR : HALO * 16 + (k + 1) * NEAR],
                 side_ref[16 * CX + k * CX : 16 * CX + (k + 1) * CX],
                 clow_ref[HALO * 16 + k * NEAR : HALO * 16 + (k + 1) * NEAR]]
        return jnp.concatenate(
            [jnp.concatenate(own, axis=0), jnp.concatenate(other, axis=0)], axis=1
        )

    for k in range(4):
        coef_ref[k * TALL : (k + 1) * TALL] = plane(k)
    diff, gate, damp, _ = coefs(coef_ref)
    mixing = [mix_ref[k] for k in range(4)]
    for f in range(2):
        planes = [plane(4 + 4 * f + k) for k in range(4)]
        for made in (3, 2, 1):
            planes = linear_step(planes, made, mixing, diff, gate, damp)
        top_ref[f] = planes[0][NEAR : NEAR + CX, 0:LANES]


def gather(mixing, nat, halo):
    return pl.pallas_call(
        gather_kernel,
        in_specs=[SM] + [VM] * 6,
        out_specs=[VM] * 2,
        out_shape=[struct(4 * TALL, RING), struct(2, CX, LANES)],
        compiler_params=params(),
        name="gather",
    )(mixing, nat, *halo)


def forcing(info_ref, hops, coef_ref, work):
    a, b, l1, l2, h1, h2 = hops
    work[0 : 4 * NEAR] = l1[...] + l2[...]
    work[4 * NEAR : 4 * (NEAR + CX)] = a[...] + b[...]
    work[4 * (NEAR + CX) : 4 * TALL] = h1[...] + h2[...]
    north = info_ref[1] == 1
    scale = coef_ref[3 * TALL : 4 * TALL]
    out = []
    for f in range(2):
        one = work[pl.ds(f, TALL, stride=4), :]
        two = work[pl.ds(2 + f, TALL, stride=4), :]
        own = jnp.where(north, two, one)
        other = jnp.where(north, one, two)
        out.append(scale * jnp.concatenate([own, other], axis=1))
    return out


def response(force, mixing, diff, gate, damp):
    planes = [force]
    for made in (2, 3):
        planes = linear_step(planes, made, mixing, diff, gate, damp)
        planes[0] = planes[0] + force
    return planes


def turn_kernel(*refs):
    info_ref, mix_ref, coef_ref, top_ref = refs[:4]
    hops, routes_hbm, w_hbm = refs[4:10], refs[10:14], refs[14]
    send_ref, resp_ref = refs[15:17]
    routes, (w, surf, count, sems, work) = refs[17:21], refs[21:]
    fetch_start(routes_hbm, routes, w_hbm, w, sems)
    send_ref[...] = jnp.zeros_like(send_ref)
    diff, gate, damp, _ = coefs(coef_ref)
    mixing = [mix_ref[k] for k in range(3)]
    force = forcing(info_ref, hops, coef_ref, work)
    for f in range(2):
        planes = response(force[f], mixing, diff, gate, damp)
        top = top_ref[f] + planes[0][NEAR : NEAR + CX, 0:LANES]
        surf[pl.ds(f, CX, stride=8), :] = rounded(top)
        for k in range(3):
            resp_ref[3 * f + k] = planes[k]

    def put(group, row, out):
        send_ref[pl.ds(group * 8 + row, 1), :] = out[0:1]
        send_ref[pl.ds(group * 8 + row + 1, 1), :] = out[1:2]

    write_contributions(routes_hbm, routes, w_hbm, w, sems, surf, count, put, None)


def turn(info, mixing, coef, top, hops, routes, weights, columns):
    pairs = weights.shape[0]
    return pl.pallas_call(
        turn_kernel,
        in_specs=[SM, SM] + [VM] * 8 + [HB] * 5,
        out_specs=[VM] * 2,
        out_shape=[struct(columns * 8, LANES), struct(6, TALL, RING)],
        scratch_shapes=pair_scratch(pairs, columns) + [pltpu.VMEM((4 * TALL, LANES), f32)],
        compiler_params=params(),
        name="turn",
    )(info, mixing, coef, top, *hops, *in_hbm(*routes, weights))


def sum_blocks(got_ref, chunk, marks, dense_ref):
    columns = got_ref.shape[0] // chunk
    for part in range(2):
        total = None
        for slot in range(2):
            k = part * 4 + slot * 2
            vals = [got_ref[pl.ds(k + f, columns, stride=chunk), :] for f in range(2)]
            vals = jnp.concatenate(vals, axis=1)
            vals = jnp.concatenate([vals, jnp.zeros((LANES - columns, RING), f32)], axis=0)
            seg = (part * 2 + slot) * CX
            here = exact_dot(marks[seg : seg + CX], vals)
            total = here if total is None else total + here
        for f in range(2):
            dense_ref[pl.ds(part * 2 + f, CX, stride=4), :] = total[:, f * LANES : (f + 1) * LANES]


def first_dense_kernel(got_ref, dense_ref, marks_ref):
    columns = got_ref.shape[0] // 9
    marks = got_ref[pl.ds(8, columns, stride=9), :]
    marks = jnp.concatenate([marks, jnp.zeros((LANES - columns, LANES), f32)], axis=0).T
    marks_ref[...] = marks[0:64]
    sum_blocks(got_ref, 9, marks, dense_ref)


def next_dense_kernel(got_ref, marks_ref, dense_ref):
    sum_blocks(got_ref, 8, marks_ref[...], dense_ref)


def densify(got, marks):
    first = marks is None
    out = struct(64, LANES)
    return pl.pallas_call(
        first_dense_kernel if first else next_dense_kernel,
        in_specs=[VM] if first else [VM, VM],
        out_specs=[VM, VM] if first else VM,
        out_shape=[out, out] if first else out,
        compiler_params=params(),
        name="densify",
    )(*([got] if first else [got, marks]))


def widen(own, other):
    return jnp.concatenate([other[120:128], own, other[0:8]], axis=0)


def bulk_kernel(
    mixrow_ref, mix_ref, cells_ref, coef_ref, resp_ref,
    low_ref, high_ref, side_ref, clow_ref, chigh_ref,
    out_ref, fa, fb, diff, gate, self_, work,
):
    lanes = lax.broadcasted_iota(jnp.int32, (1, LANES), 1)
    level = jnp.where(lanes >= LEV, lanes - LEV, lanes)
    mix = mixrow_ref[...]
    mix_up = jnp.where(level == LEV - 1, 0.0, mix)
    mix_low = jnp.where(level == 0, 0.0, mix)
    mix_mid = -(mix_up + mix_low)

    for x in range(CX):
        fa[HALO + x, 16:144] = cells_ref[x]
        fa[HALO + x, 8:16] = side_ref[16 * x + 8 : 16 * x + 16]
        fa[HALO + x, 144:152] = side_ref[16 * x : 16 * x + 8]
    for j in range(HALO):
        for at, along, corner in ((j, high_ref, chigh_ref), (HALO + CX + j, low_ref, clow_ref)):
            fa[at, 16:144] = along[j * LANES : (j + 1) * LANES]
            fa[at, 8:16] = corner[16 * j + 8 : 16 * j + 16]
            fa[at, 144:152] = corner[16 * j : 16 * j + 8]

    work[...] = jnp.zeros_like(work)

    def columns_of(one, two):
        wide = []
        for part in range(2):
            at = slice(part * LANES, (part + 1) * LANES)
            work[0:TALL] = coef_ref[one * TALL : (one + 1) * TALL, at]
            work[64 : 64 + TALL] = coef_ref[two * TALL : (two + 1) * TALL, at]
            wide.append(work[...].T)
        return widen(*wide)

    both = columns_of(0, 1)
    damping = columns_of(2, 2)
    for i in range(CX + 2 * HALO - 2):
        at = i + NEAR - HALO + 1
        d = jnp.broadcast_to(both[:, at : at + 1], (WIDE, LANES))
        g = jnp.broadcast_to(both[:, 64 + at : 65 + at], (WIDE, LANES))
        damp = jnp.where(level == 0, pltpu.roll(damping, LANES - at, 1), 0.0)
        diff[i] = d
        gate[i] = g
        self_[i] = (1.0 - 4.0 * d) + (g * mix_mid - damp)

    def advance(src, dst, x):
        for y in range(8, 8 + WIDE, CHUNK):
            at = slice(y, y + CHUNK)
            k = slice(y - 8, y - 8 + CHUNK)
            c = src[x, at]
            near = (src[x - 1, at] + src[x + 1, at]) + (
                src[x, y - 1 : y - 1 + CHUNK] + src[x, y + 1 : y + 1 + CHUNK]
            )
            vert = mix_up * pltpu.roll(c, LANES - 1, 1) + mix_low * pltpu.roll(c, 1, 1)
            dst[x, at] = self_[x - 1, k] * c + diff[x - 1, k] * near + gate[x - 1, k] * vert

    src, dst = fa, fb
    for step in range(1, HALO + 1):

        def body(x, carry, src=src, dst=dst):
            advance(src, dst, x)
            return carry

        lax.fori_loop(step, CX + 2 * HALO - step, body, 0, unroll=True)
        src, dst = dst, src
    for x in range(CX):
        out_ref[pl.ds(x, LANES, stride=CX), :] = src[HALO + x, 16:144].T

    d, g, c, _ = coefs(coef_ref)
    mixing = [mix_ref[k] for k in range(6)]
    for f in range(2):
        planes = [resp_ref[3 * f + k] for k in range(3)]
        for made in (4, 5, 6):
            planes = linear_step(planes, made, mixing, d, g, c)
        for k in range(6):
            at = (f * LEV + k) * CX
            out_ref[at : at + CX] += planes[k][NEAR : NEAR + CX, 0:LANES]


def bulk(mixrow, mixing, cells, coef, resp, halo):
    big = pltpu.VMEM((CX + 2 * HALO, WIDE + 16, LANES), f32)
    coefficient = pltpu.VMEM((CX + 2 * HALO - 2, WIDE, LANES), f32)
    return pl.pallas_call(
        bulk_kernel,
        in_specs=[VM, SM] + [VM] * 8,
        out_specs=VM,
        out_shape=struct(2 * LEV * CX, LANES),
        scratch_shapes=[big, big] + [coefficient] * 3 + [pltpu.VMEM((LANES, LANES), f32)],
        compiler_params=params(),
        cost_estimate=pl.CostEstimate(flops=40_000_000, transcendentals=0, bytes_accessed=40_000_000),
        name="bulk",
    )(mixrow, mixing, cells, coef, resp, *halo)


def final_kernel(info_ref, mix_ref, coef_ref, a, b, l1, l2, h1, h2, part_ref, out_ref, work):
    diff, gate, damp, _ = coefs(coef_ref)
    mixing = [mix_ref[k] for k in range(3)]
    force = forcing(info_ref, (a, b, l1, l2, h1, h2), coef_ref, work)
    for f in range(2):
        planes = response(force[f], mixing, diff, gate, damp)
        for k in range(3):
            out_ref[f, k] = part_ref[f, k] + planes[k][NEAR : NEAR + CX, 0:LANES]


def final(info, mixing, coef, hops, part):
    block = pl.BlockSpec((2, 3, CX, LANES), lambda i: (0, 0, 0, 0))
    return pl.pallas_call(
        final_kernel,
        grid=(1,),
        in_specs=[SM, SM] + [VM] * 7 + [block],
        out_specs=block,
        out_shape=struct(2, LEV, CX, LANES),
        input_output_aliases={9: 0},
        scratch_shapes=[pltpu.VMEM((4 * TALL, LANES), f32)],
        compiler_params=params(),
        name="final",
    )(info, mixing, coef, *hops, part)


def solution(mesh):
    comps, columns, halves = (mesh.shape[a] for a in AXES)

    def sent(value, where):
        pairs = []
        for s in range(comps):
            for g in range(columns):
                for h in range(halves):
                    a, b, c = where(s, g, h)
                    b, c = b % columns, c % halves
                    pairs.append(((s * columns + g) * halves + h, (a * columns + b) * halves + c))
        return lax.ppermute(value, AXES, pairs)

    def exchanged(low, high, side, clow, chigh):
        return (
            sent(low, lambda s, g, h: (s, g - 1, h)),
            sent(high, lambda s, g, h: (s, g + 1, h)),
            sent(side, lambda s, g, h: (s, g, h + 1)),
            sent(clow, lambda s, g, h: (s, g - 1, h + 1)),
            sent(chigh, lambda s, g, h: (s, g + 1, h + 1)),
        )

    def hopped(dense):
        first, final_ = dense[: 4 * NEAR], dense[4 * (CX - NEAR) :]
        return (
            sent(dense, lambda s, g, h: (1 - s, g, h)),
            sent(dense, lambda s, g, h: (1 - s, g, h + 1)),
            sent(final_, lambda s, g, h: (1 - s, g + 1, h)),
            sent(final_, lambda s, g, h: (1 - s, g + 1, h + 1)),
            sent(first, lambda s, g, h: (1 - s, g - 1, h)),
            sent(first, lambda s, g, h: (1 - s, g - 1, h + 1)),
        )

    def body(
        state, diffusion, vertical, coupling, land_sea,
        route_tile, route_src, route_dst, pair_cols, intersection,
    ):
        info = jnp.stack([lax.axis_index("comp"), lax.axis_index("gy")]).astype(jnp.int32)
        mixing = vertical[0]
        mixrow = jnp.concatenate([vertical, vertical], axis=1)
        routes = (route_tile[0, 0, :, 0], route_src[0, 0], route_dst[0, 0], pair_cols[0, 0])
        weights = intersection[0, 0]

        send = first_contributions(routes, weights, state[0], columns)
        got = lax.all_to_all(send, "gx", 0, 0, tiled=True)
        cells, nat, *edges = prepare(
            info, state.reshape(-1, LANES), diffusion[0], coupling[0], land_sea[0]
        )
        halo = exchanged(*edges)
        coef, top = gather(mixing, nat, halo)
        dense, marks = densify(got.reshape(-1, LANES), None)
        hops = hopped(dense)
        send, resp = turn(info, mixing, coef, top, hops, routes, weights, columns)

        got = lax.all_to_all(send, "gx", 0, 0, tiled=True)
        part = bulk(mixrow, mixing, cells, coef, resp, halo)
        got, part = lax.optimization_barrier((got, part))
        hops = hopped(densify(got, marks))
        out = final(info, mixing, coef, hops, part.reshape(state.shape[1:]))
        return out[None]

    spec = P("comp", "gx", "gy")
    route = P("comp", ("gx", "gy"))
    return jax.shard_map(
        body,
        mesh=mesh,
        in_specs=(
            P("comp", None, None, "gx", "gy"), spec, P("comp", None), spec, spec,
            route, route, route, route, route,
        ),
        out_specs=P("comp", None, None, "gx", "gy"),
        check_vma=False,
    )
```

```python
import jax
import jax.numpy as jnp
from jax import lax
from jax.experimental import pallas as pl
from jax.experimental.pallas import tpu as pltpu
from jax.sharding import PartitionSpec as P

LANES = 128
LEV = 64
CX = 16
WIDE = 144
HALO = 6
CHUNK = 48
NEAR = 8
TALL = CX + 2 * NEAR
RING = 2 * LANES
NAT = 12
AXES = ("comp", "gx", "gy")
VMEM_LIMIT = 48 * 2**20

f32 = jnp.float32
VM = pl.BlockSpec(memory_space=pltpu.VMEM)
SM = pl.BlockSpec(memory_space=pltpu.SMEM)
HB = pl.BlockSpec(memory_space=pltpu.HBM)


def params():
    return pltpu.CompilerParams(vmem_limit_bytes=VMEM_LIMIT)


def struct(*shape):
    return jax.ShapeDtypeStruct(shape, f32)


def in_hbm(*arrays):
    return [pltpu.with_memory_space_constraint(a, pltpu.HBM) for a in arrays]


def exact_dot(a, b):
    return lax.dot_general(
        a, b, (((1,), (0,)), ((), ())), precision=lax.Precision.HIGHEST, preferred_element_type=f32
    )


PARTS = 4


def fetch_start(routes_hbm, routes, w_hbm, w, sems):
    for i in range(4):
        pltpu.make_async_copy(routes_hbm[i], routes[i], sems.at[i]).start()
    per = w.shape[0] // PARTS
    for i in range(PARTS):
        at = pl.ds(i * per, per)
        pltpu.make_async_copy(w_hbm.at[at], w.at[at], sems.at[4 + i]).start()


def write_contributions(routes_hbm, routes, w_hbm, w, sems, surf, count, put, mark):
    tile_ref, src_ref, dst_ref, cols_ref = routes
    for i in range(count.shape[0]):
        count[i] = 0
    for i in range(4):
        pltpu.make_async_copy(routes_hbm[i], routes[i], sems.at[i]).wait()
    lanes = lax.broadcasted_iota(jnp.int32, (1, LANES), 1)
    per = w.shape[0] // PARTS
    for p in range(w.shape[0]):
        if p % per == 0:
            at = pl.ds(p, per)
            pltpu.make_async_copy(w_hbm.at[at], w.at[at], sems.at[4 + p // per]).wait()
        dest = tile_ref[p]
        slot = count[dest]
        count[dest] = slot + 1
        group = dest // 2
        part = dest - 2 * group
        picked = surf[pl.ds(pl.multiple_of(src_ref[p] * 8, 8), 8), :].astype(jnp.bfloat16)
        out = lax.dot_general(
            picked, w[p], (((1,), (1,)), ((), ())), preferred_element_type=f32
        )
        out = jnp.where(lanes < cols_ref[p], out, 0.0)
        put(group, part * 4 + slot * 2, out)
        if mark is not None:
            hot = (part * 2 + slot) * CX + dst_ref[p]
            mark(group, jnp.where(lanes == hot, 1.0, 0.0))


def pair_scratch(pairs, columns):
    return [pltpu.SMEM((pairs,), jnp.int32)] * 4 + [
        pltpu.VMEM((pairs, LANES, LANES), jnp.bfloat16),
        pltpu.VMEM((LANES, LANES), f32),
        pltpu.SMEM((2 * columns,), jnp.int32),
        pltpu.SemaphoreType.DMA((4 + PARTS,)),
    ]


def rounded(x):
    return x.astype(jnp.bfloat16).astype(f32)


def first_kernel(*refs):
    routes_hbm, w_hbm, state_hbm, send_ref = refs[:4], refs[4], refs[5], refs[6]
    routes, (w, surf, count, sems, top, top_sems) = refs[7:11], refs[11:]
    tops = [
        pltpu.make_async_copy(state_hbm.at[f, 0], top.at[f], top_sems.at[f]) for f in range(2)
    ]
    for copy in tops:
        copy.start()
    fetch_start(routes_hbm, routes, w_hbm, w, sems)
    send_ref[...] = jnp.zeros_like(send_ref)
    for f in range(2):
        tops[f].wait()
        surf[pl.ds(f, CX, stride=8), :] = rounded(top[f])

    def put(group, row, out):
        send_ref[group * 9 + row] = out[0:1]
        send_ref[group * 9 + row + 1] = out[1:2]

    def mark(group, value):
        send_ref[group * 9 + 8] += value

    write_contributions(routes_hbm, routes, w_hbm, w, sems, surf, count, put, mark)


def first_contributions(routes, weights, state, columns):
    pairs = weights.shape[0]
    return pl.pallas_call(
        first_kernel,
        in_specs=[HB] * 6,
        out_specs=VM,
        out_shape=struct(columns * 9, 1, LANES),
        scratch_shapes=pair_scratch(pairs, columns)
        + [pltpu.VMEM((2, CX, LANES), f32), pltpu.SemaphoreType.DMA((2,))],
        compiler_params=params(),
        name="contrib",
    )(*in_hbm(*routes, weights, state))


EDGE = HALO * LANES
EDGE_NAT = EDGE + NAT * NEAR
EDGE_ROWS = EDGE_NAT + NAT * NEAR + HALO * 16
SIDE = NAT * NEAR
SIDE_NAT = SIDE + 16 * CX
SIDE_ROWS = SIDE_NAT + NAT * NEAR
CORNER = NAT * NEAR + HALO * 16


def prepare_kernel(
    info_ref, state_hbm, diff_hbm, coup_hbm, sea_hbm, cells_ref, nat_ref, side_ref,
    state_ref, diff_ref, coup_ref, sea_ref, sems,
):
    copies = [
        pltpu.make_async_copy(a, b, sems.at[i])
        for i, (a, b) in enumerate(
            ((diff_hbm, diff_ref), (coup_hbm, coup_ref), (sea_hbm, sea_ref), (state_hbm, state_ref))
        )
    ]
    for copy in copies:
        copy.start()
    for copy in copies[:3]:
        copy.wait()
    sea = sea_ref[...].astype(f32)
    gate = jnp.where(info_ref[0] == 1, sea, jnp.ones_like(sea))
    coup = gate * coup_ref[...]
    nat_ref[0:16] = gate * diff_ref[...]
    nat_ref[16:32] = gate
    nat_ref[32:48] = coup
    nat_ref[48:64] = coup * sea
    copies[3].wait()
    for f in range(2):
        nat_ref[64 * (f + 1) : 64 * (f + 2)] = state_ref[f * LEV * CX : f * LEV * CX + 64]
    for k in range(NAT):
        at = k * NEAR
        side_ref[at : at + NEAR] = nat_ref[k * CX : k * CX + NEAR]
        side_ref[SIDE_NAT + at : SIDE_NAT + at + NEAR] = nat_ref[(k + 1) * CX - NEAR : (k + 1) * CX]
    for x in range(CX):
        row = state_ref[pl.ds(x, LANES, stride=CX), :].T
        cells_ref[x] = row
        at = SIDE + 16 * x
        side_ref[at : at + 8] = row[0:8]
        side_ref[at + 8 : at + 16] = row[120:128]


def prepare(info, state, diffusion, coupling, land_sea):
    tile = pltpu.VMEM((CX, LANES), f32)
    return pl.pallas_call(
        prepare_kernel,
        in_specs=[SM] + [HB] * 4,
        out_specs=[VM] * 3,
        out_shape=[
            struct(CX, LANES, LANES), struct(NAT * CX, LANES), struct(SIDE_ROWS, LANES),
        ],
        scratch_shapes=[
            pltpu.VMEM(state.shape, f32), tile, tile, pltpu.VMEM((CX, LANES), jnp.int32),
            pltpu.SemaphoreType.DMA((4,)),
        ],
        compiler_params=params(),
        name="prepare",
    )(info, *in_hbm(state, diffusion, coupling, land_sea))


def pack_kernel(cells_ref, nat_ref, side_ref, low_ref, high_ref):
    for j in range(HALO):
        low_ref[j * LANES : (j + 1) * LANES] = cells_ref[j]
        high_ref[j * LANES : (j + 1) * LANES] = cells_ref[CX - HALO + j]
    for k in range(NAT):
        at = EDGE + k * NEAR
        low_ref[at : at + NEAR] = nat_ref[k * CX : k * CX + NEAR]
        high_ref[at : at + NEAR] = nat_ref[(k + 1) * CX - NEAR : (k + 1) * CX]
    low_ref[EDGE_NAT:] = side_ref[0:CORNER]
    high_ref[EDGE_NAT:] = side_ref[SIDE_ROWS - CORNER :]


def pack(cells, nat, side):
    return pl.pallas_call(
        pack_kernel,
        in_specs=[VM] * 3,
        out_specs=[VM] * 2,
        out_shape=[struct(EDGE_ROWS, LANES)] * 2,
        compiler_params=params(),
        name="pack",
    )(cells, nat, side)


def linear_step(planes, made, mixing, diff, gate, damp):
    out = []
    for k in range(made):
        c = planes[k] if k < len(planes) else None
        vert = None

        def add(total, term):
            return term if total is None else total + term

        m = mixing[k]
        if k + 1 < len(planes):
            vert = add(vert, m * planes[k + 1])
        if k > 0:
            vert = add(vert, m * planes[k - 1])
        if c is None:
            out.append(gate * vert)
            continue
        vert = add(vert, -(m if k == 0 else 2.0 * m) * c)
        lap = (
            pltpu.roll(c, 1, 0) + pltpu.roll(c, TALL - 1, 0)
            + pltpu.roll(c, 1, 1) + pltpu.roll(c, RING - 1, 1) - 4.0 * c
        )
        new = c + (diff * lap + gate * vert)
        out.append(new - damp * c if k == 0 else new)
    return out


def coefs(coef_ref):
    return [coef_ref[k * TALL : (k + 1) * TALL] for k in range(4)]


def gather_kernel(mix_ref, nat_ref, low_ref, high_ref, side_ref, coef_ref, top_ref):
    def plane(k):
        def part(ref, base):
            return ref[base + k * NEAR : base + (k + 1) * NEAR]

        own = [part(high_ref, EDGE), nat_ref[k * CX : (k + 1) * CX], part(low_ref, EDGE)]
        other = [
            part(high_ref, EDGE_NAT + HALO * 16), part(side_ref, 0), part(side_ref, SIDE_NAT),
            part(low_ref, EDGE_NAT),
        ]
        return jnp.concatenate(
            [jnp.concatenate(own, axis=0), jnp.concatenate(other, axis=0)], axis=1
        )

    for k in range(4):
        coef_ref[k * TALL : (k + 1) * TALL] = plane(k)
    diff, gate, damp, _ = coefs(coef_ref)
    mixing = [mix_ref[k] for k in range(4)]
    for f in range(2):
        planes = [plane(4 + 4 * f + k) for k in range(4)]
        for made in (3, 2, 1):
            planes = linear_step(planes, made, mixing, diff, gate, damp)
        top_ref[f] = planes[0][NEAR : NEAR + CX, 0:LANES]


def gather(mixing, nat, halo):
    return pl.pallas_call(
        gather_kernel,
        in_specs=[SM] + [VM] * 4,
        out_specs=[VM] * 2,
        out_shape=[struct(4 * TALL, RING), struct(2, CX, LANES)],
        compiler_params=params(),
        name="gather",
    )(mixing, nat, *halo)


def forcing(info_ref, hops, coef_ref, work):
    own, low, high = hops
    work[0 : 4 * NEAR] = low[...]
    work[4 * NEAR : 4 * (NEAR + CX)] = own[...]
    work[4 * (NEAR + CX) : 4 * TALL] = high[...]
    north = info_ref[1] == 1
    scale = coef_ref[3 * TALL : 4 * TALL]
    out = []
    for f in range(2):
        one = work[pl.ds(f, TALL, stride=4), :]
        two = work[pl.ds(2 + f, TALL, stride=4), :]
        own = jnp.where(north, two, one)
        other = jnp.where(north, one, two)
        out.append(scale * jnp.concatenate([own, other], axis=1))
    return out


def response(force, mixing, diff, gate, damp):
    planes = [force]
    for made in (2, 3):
        planes = linear_step(planes, made, mixing, diff, gate, damp)
        planes[0] = planes[0] + force
    return planes


def turn_kernel(*refs):
    info_ref, mix_ref, coef_ref, top_ref = refs[:4]
    hops, routes_hbm, w_hbm = refs[4:7], refs[7:11], refs[11]
    send_ref, resp_ref = refs[12:14]
    routes, (w, surf, count, sems, work) = refs[14:18], refs[18:]
    fetch_start(routes_hbm, routes, w_hbm, w, sems)
    send_ref[...] = jnp.zeros_like(send_ref)
    diff, gate, damp, _ = coefs(coef_ref)
    mixing = [mix_ref[k] for k in range(3)]
    force = forcing(info_ref, hops, coef_ref, work)
    for f in range(2):
        planes = response(force[f], mixing, diff, gate, damp)
        top = top_ref[f] + planes[0][NEAR : NEAR + CX, 0:LANES]
        surf[pl.ds(f, CX, stride=8), :] = rounded(top)
        for k in range(3):
            resp_ref[3 * f + k] = planes[k]

    def put(group, row, out):
        send_ref[pl.ds(group * 8 + row, 1), :] = out[0:1]
        send_ref[pl.ds(group * 8 + row + 1, 1), :] = out[1:2]

    write_contributions(routes_hbm, routes, w_hbm, w, sems, surf, count, put, None)


def turn(info, mixing, coef, top, hops, routes, weights, columns):
    pairs = weights.shape[0]
    return pl.pallas_call(
        turn_kernel,
        in_specs=[SM, SM] + [VM] * 5 + [HB] * 5,
        out_specs=[VM] * 2,
        out_shape=[struct(columns * 8, LANES), struct(6, TALL, RING)],
        scratch_shapes=pair_scratch(pairs, columns) + [pltpu.VMEM((4 * TALL, LANES), f32)],
        compiler_params=params(),
        name="turn",
    )(info, mixing, coef, top, *hops, *in_hbm(*routes, weights))


def sum_blocks(got_ref, chunk, marks, dense_ref):
    columns = got_ref.shape[0] // chunk
    for part in range(2):
        total = None
        for slot in range(2):
            k = part * 4 + slot * 2
            vals = [got_ref[pl.ds(k + f, columns, stride=chunk), :] for f in range(2)]
            vals = jnp.concatenate(vals, axis=1)
            vals = jnp.concatenate([vals, jnp.zeros((LANES - columns, RING), f32)], axis=0)
            seg = (part * 2 + slot) * CX
            here = exact_dot(marks[seg : seg + CX], vals)
            total = here if total is None else total + here
        for f in range(2):
            dense_ref[pl.ds(part * 2 + f, CX, stride=4), :] = total[:, f * LANES : (f + 1) * LANES]


def first_dense_kernel(got_ref, dense_ref, marks_ref):
    columns = got_ref.shape[0] // 9
    marks = got_ref[pl.ds(8, columns, stride=9), :]
    marks = jnp.concatenate([marks, jnp.zeros((LANES - columns, LANES), f32)], axis=0).T
    marks_ref[...] = marks[0:64]
    sum_blocks(got_ref, 9, marks, dense_ref)


def next_dense_kernel(got_ref, marks_ref, dense_ref):
    sum_blocks(got_ref, 8, marks_ref[...], dense_ref)


def densify(got, marks):
    first = marks is None
    out = struct(64, LANES)
    return pl.pallas_call(
        first_dense_kernel if first else next_dense_kernel,
        in_specs=[VM] if first else [VM, VM],
        out_specs=[VM, VM] if first else VM,
        out_shape=[out, out] if first else out,
        compiler_params=params(),
        name="densify",
    )(*([got] if first else [got, marks]))


def widen(own, other):
    return jnp.concatenate([other[120:128], own, other[0:8]], axis=0)


def bulk_kernel(
    mixrow_ref, mix_ref, cells_ref, coef_ref, resp_ref,
    low_ref, high_ref, side_ref,
    out_ref, top_ref, fa, fb, diff, gate, self_, work,
):
    lanes = lax.broadcasted_iota(jnp.int32, (1, LANES), 1)
    level = jnp.where(lanes >= LEV, lanes - LEV, lanes)
    mix = mixrow_ref[...]
    mix_up = jnp.where(level == LEV - 1, 0.0, mix)
    mix_low = jnp.where(level == 0, 0.0, mix)
    mix_mid = -(mix_up + mix_low)

    for x in range(CX):
        fa[HALO + x, 16:144] = cells_ref[x]
        fa[HALO + x, 8:16] = side_ref[SIDE + 16 * x + 8 : SIDE + 16 * x + 16]
        fa[HALO + x, 144:152] = side_ref[SIDE + 16 * x : SIDE + 16 * x + 8]
    for j in range(HALO):
        for at, along, base in ((j, high_ref, EDGE_NAT), (HALO + CX + j, low_ref, EDGE_NAT + NAT * NEAR)):
            fa[at, 16:144] = along[j * LANES : (j + 1) * LANES]
            fa[at, 8:16] = along[base + 16 * j + 8 : base + 16 * j + 16]
            fa[at, 144:152] = along[base + 16 * j : base + 16 * j + 8]

    work[...] = jnp.zeros_like(work)

    def columns_of(one, two):
        wide = []
        for part in range(2):
            at = slice(part * LANES, (part + 1) * LANES)
            work[0:TALL] = coef_ref[one * TALL : (one + 1) * TALL, at]
            work[64 : 64 + TALL] = coef_ref[two * TALL : (two + 1) * TALL, at]
            wide.append(work[...].T)
        return widen(*wide)

    both = columns_of(0, 1)
    damping = columns_of(2, 2)
    for i in range(CX + 2 * HALO - 2):
        at = i + NEAR - HALO + 1
        d = jnp.broadcast_to(both[:, at : at + 1], (WIDE, LANES))
        g = jnp.broadcast_to(both[:, 64 + at : 65 + at], (WIDE, LANES))
        damp = jnp.where(level == 0, pltpu.roll(damping, LANES - at, 1), 0.0)
        diff[i] = d
        gate[i] = g
        self_[i] = (1.0 - 4.0 * d) + (g * mix_mid - damp)

    def advance(src, dst, x):
        for y in range(8, 8 + WIDE, CHUNK):
            at = slice(y, y + CHUNK)
            k = slice(y - 8, y - 8 + CHUNK)
            c = src[x, at]
            near = (src[x - 1, at] + src[x + 1, at]) + (
                src[x, y - 1 : y - 1 + CHUNK] + src[x, y + 1 : y + 1 + CHUNK]
            )
            vert = mix_up * pltpu.roll(c, LANES - 1, 1) + mix_low * pltpu.roll(c, 1, 1)
            dst[x, at] = self_[x - 1, k] * c + diff[x - 1, k] * near + gate[x - 1, k] * vert

    src, dst = fa, fb
    for step in range(1, HALO + 1):

        def body(x, carry, src=src, dst=dst):
            advance(src, dst, x)
            return carry

        lax.fori_loop(step, CX + 2 * HALO - step, body, 0, unroll=True)
        src, dst = dst, src
    for x in range(CX):
        out_ref[pl.ds(x, LANES, stride=CX), :] = src[HALO + x, 16:144].T

    d, g, c, _ = coefs(coef_ref)
    mixing = [mix_ref[k] for k in range(6)]
    for f in range(2):
        planes = [resp_ref[3 * f + k] for k in range(3)]
        for made in (4, 5, 6):
            planes = linear_step(planes, made, mixing, d, g, c)
        for k in range(6):
            at = (f * LEV + k) * CX
            full = out_ref[at : at + CX] + planes[k][NEAR : NEAR + CX, 0:LANES]
            out_ref[at : at + CX] = full
            if k < 3:
                top_ref[f, k] = full


def bulk(mixrow, mixing, cells, coef, resp, halo):
    big = pltpu.VMEM((CX + 2 * HALO, WIDE + 16, LANES), f32)
    coefficient = pltpu.VMEM((CX + 2 * HALO - 2, WIDE, LANES), f32)
    return pl.pallas_call(
        bulk_kernel,
        in_specs=[VM, SM] + [VM] * 6,
        out_specs=[VM, VM],
        out_shape=[struct(2 * LEV * CX, LANES), struct(2, 3, CX, LANES)],
        scratch_shapes=[big, big] + [coefficient] * 3 + [pltpu.VMEM((LANES, LANES), f32)],
        compiler_params=params(),
        cost_estimate=pl.CostEstimate(flops=40_000_000, transcendentals=0, bytes_accessed=40_000_000),
        name="bulk",
    )(mixrow, mixing, cells, coef, resp, *halo)


def final_kernel(info_ref, mix_ref, coef_ref, own, low, high, top_ref, part_ref, out_ref, work):
    diff, gate, damp, _ = coefs(coef_ref)
    mixing = [mix_ref[k] for k in range(3)]
    force = forcing(info_ref, (own, low, high), coef_ref, work)
    for f in range(2):
        planes = response(force[f], mixing, diff, gate, damp)
        for k in range(3):
            out_ref[f, k] = top_ref[f, k] + planes[k][NEAR : NEAR + CX, 0:LANES]


def final(info, mixing, coef, hops, top, part):
    block = pl.BlockSpec((2, 3, CX, LANES), lambda i: (0, 0, 0, 0))
    return pl.pallas_call(
        final_kernel,
        grid=(1,),
        in_specs=[SM, SM] + [VM] * 5 + [HB],
        out_specs=block,
        out_shape=struct(2, LEV, CX, LANES),
        input_output_aliases={7: 0},
        scratch_shapes=[pltpu.VMEM((4 * TALL, LANES), f32)],
        compiler_params=params(),
        name="final",
    )(info, mixing, coef, *hops, top, part)


def solution(mesh):
    comps, columns, halves = (mesh.shape[a] for a in AXES)

    def sent(value, where):
        pairs = []
        for s in range(comps):
            for g in range(columns):
                for h in range(halves):
                    a, b, c = where(s, g, h)
                    b, c = b % columns, c % halves
                    pairs.append(((s * columns + g) * halves + h, (a * columns + b) * halves + c))
        return lax.ppermute(value, AXES, pairs)

    def hopped(dense):
        full = dense + sent(dense, lambda s, g, h: (s, g, h + 1))
        return (
            sent(full, lambda s, g, h: (1 - s, g, h)),
            sent(full[4 * (CX - NEAR) :], lambda s, g, h: (1 - s, g + 1, h)),
            sent(full[: 4 * NEAR], lambda s, g, h: (1 - s, g - 1, h)),
        )

    def body(
        state, diffusion, vertical, coupling, land_sea,
        route_tile, route_src, route_dst, pair_cols, intersection,
    ):
        info = jnp.stack([lax.axis_index("comp"), lax.axis_index("gy")]).astype(jnp.int32)
        mixing = vertical[0]
        mixrow = jnp.concatenate([vertical, vertical], axis=1)
        routes = (route_tile[0, 0, :, 0], route_src[0, 0], route_dst[0, 0], pair_cols[0, 0])
        weights = intersection[0, 0]

        cells, nat, side = prepare(
            info, state.reshape(-1, LANES), diffusion[0], coupling[0], land_sea[0]
        )
        side = sent(side, lambda s, g, h: (s, g, h + 1))
        send = first_contributions(routes, weights, state[0], columns)
        send, side = lax.optimization_barrier((send, side))
        got = lax.all_to_all(send, "gx", 0, 0, tiled=True)
        low, high = pack(cells, nat, side)
        halo = (
            sent(low, lambda s, g, h: (s, g - 1, h)),
            sent(high, lambda s, g, h: (s, g + 1, h)),
            side,
        )
        coef, top = gather(mixing, nat, halo)
        dense, marks = densify(got.reshape(-1, LANES), None)
        hops = hopped(dense)
        send, resp = turn(info, mixing, coef, top, hops, routes, weights, columns)

        got = lax.all_to_all(send, "gx", 0, 0, tiled=True)
        part, low = bulk(mixrow, mixing, cells, coef, resp, halo)
        got, part, low = lax.optimization_barrier((got, part, low))
        hops = hopped(densify(got, marks))
        out = final(info, mixing, coef, hops, low, part.reshape(state.shape[1:]))
        return out[None]

    spec = P("comp", "gx", "gy")
    route = P("comp", ("gx", "gy"))
    return jax.shard_map(
        body,
        mesh=mesh,
        in_specs=(
            P("comp", None, None, "gx", "gy"), spec, P("comp", None), spec, spec,
            route, route, route, route, route,
        ),
        out_specs=P("comp", None, None, "gx", "gy"),
        check_vma=False,
    )
```

```python
import jax
import jax.numpy as jnp
from jax import lax
from jax.experimental import pallas as pl
from jax.experimental.pallas import tpu as pltpu
from jax.sharding import PartitionSpec as P

LANES = 128
LEV = 64
CX = 16
WIDE = 144
HALO = 6
CHUNK = 48
NEAR = 8
TALL = CX + 2 * NEAR
RING = 2 * LANES
NAT = 12
AXES = ("comp", "gx", "gy")
VMEM_LIMIT = 48 * 2**20

f32 = jnp.float32
VM = pl.BlockSpec(memory_space=pltpu.VMEM)
SM = pl.BlockSpec(memory_space=pltpu.SMEM)
HB = pl.BlockSpec(memory_space=pltpu.HBM)


def params():
    return pltpu.CompilerParams(vmem_limit_bytes=VMEM_LIMIT)


def struct(*shape):
    return jax.ShapeDtypeStruct(shape, f32)


def in_hbm(*arrays):
    return [pltpu.with_memory_space_constraint(a, pltpu.HBM) for a in arrays]


def exact_dot(a, b):
    return lax.dot_general(
        a, b, (((1,), (0,)), ((), ())), precision=lax.Precision.HIGHEST, preferred_element_type=f32
    )


PARTS = 4


def fetch_start(routes_hbm, routes, w_hbm, w, sems):
    for i in range(4):
        pltpu.make_async_copy(routes_hbm[i], routes[i], sems.at[i]).start()
    per = w.shape[0] // PARTS
    for i in range(PARTS):
        at = pl.ds(i * per, per)
        pltpu.make_async_copy(w_hbm.at[at], w.at[at], sems.at[4 + i]).start()


def write_contributions(routes_hbm, routes, w_hbm, w, sems, surf, count, put, mark):
    tile_ref, src_ref, dst_ref, cols_ref = routes
    for i in range(count.shape[0]):
        count[i] = 0
    for i in range(4):
        pltpu.make_async_copy(routes_hbm[i], routes[i], sems.at[i]).wait()
    lanes = lax.broadcasted_iota(jnp.int32, (1, LANES), 1)
    per = w.shape[0] // PARTS
    for p in range(w.shape[0]):
        if p % per == 0:
            at = pl.ds(p, per)
            pltpu.make_async_copy(w_hbm.at[at], w.at[at], sems.at[4 + p // per]).wait()
        dest = tile_ref[p]
        slot = count[dest]
        count[dest] = slot + 1
        group = dest // 2
        part = dest - 2 * group
        picked = surf[pl.ds(pl.multiple_of(src_ref[p] * 8, 8), 8), :].astype(jnp.bfloat16)
        out = lax.dot_general(
            picked, w[p], (((1,), (1,)), ((), ())), preferred_element_type=f32
        )
        out = jnp.where(lanes < cols_ref[p], out, 0.0)
        put(group, part * 4 + slot * 2, out)
        if mark is not None:
            hot = (part * 2 + slot) * CX + dst_ref[p]
            mark(group, jnp.where(lanes == hot, 1.0, 0.0))


def pair_scratch(pairs, columns):
    return [pltpu.SMEM((pairs,), jnp.int32)] * 4 + [
        pltpu.VMEM((pairs, LANES, LANES), jnp.bfloat16),
        pltpu.VMEM((LANES, LANES), f32),
        pltpu.SMEM((2 * columns,), jnp.int32),
        pltpu.SemaphoreType.DMA((4 + PARTS,)),
    ]


def rounded(x):
    return x.astype(jnp.bfloat16).astype(f32)


def first_kernel(*refs):
    routes_hbm, w_hbm, state_hbm, send_ref = refs[:4], refs[4], refs[5], refs[6]
    routes, (w, surf, count, sems, top, top_sems) = refs[7:11], refs[11:]
    tops = [
        pltpu.make_async_copy(state_hbm.at[f, 0], top.at[f], top_sems.at[f]) for f in range(2)
    ]
    for copy in tops:
        copy.start()
    fetch_start(routes_hbm, routes, w_hbm, w, sems)
    send_ref[...] = jnp.zeros_like(send_ref)
    for f in range(2):
        tops[f].wait()
        surf[pl.ds(f, CX, stride=8), :] = rounded(top[f])

    def put(group, row, out):
        send_ref[group * 9 + row] = out[0:1]
        send_ref[group * 9 + row + 1] = out[1:2]

    def mark(group, value):
        send_ref[group * 9 + 8] += value

    write_contributions(routes_hbm, routes, w_hbm, w, sems, surf, count, put, mark)


def first_contributions(routes, weights, state, columns):
    pairs = weights.shape[0]
    return pl.pallas_call(
        first_kernel,
        in_specs=[HB] * 6,
        out_specs=VM,
        out_shape=struct(columns * 9, 1, LANES),
        scratch_shapes=pair_scratch(pairs, columns)
        + [pltpu.VMEM((2, CX, LANES), f32), pltpu.SemaphoreType.DMA((2,))],
        compiler_params=params(),
        name="contrib",
    )(*in_hbm(*routes, weights, state))


EDGE = HALO * LANES
EDGE_NAT = EDGE + NAT * NEAR
EDGE_ROWS = EDGE_NAT + NAT * NEAR + HALO * 2 * HALO
SIDE = NAT * NEAR
SIDE_NAT = SIDE + 2 * HALO * CX
SIDE_ROWS = SIDE_NAT + NAT * NEAR
CORNER = NAT * NEAR + HALO * 2 * HALO


def prepare_kernel(
    info_ref, state_hbm, diff_hbm, coup_hbm, sea_hbm, cells_ref, nat_ref, side_ref,
    state_ref, diff_ref, coup_ref, sea_ref, sems,
):
    copies = [
        pltpu.make_async_copy(a, b, sems.at[i])
        for i, (a, b) in enumerate(
            ((diff_hbm, diff_ref), (coup_hbm, coup_ref), (sea_hbm, sea_ref), (state_hbm, state_ref))
        )
    ]
    for copy in copies:
        copy.start()
    for copy in copies[:3]:
        copy.wait()
    sea = sea_ref[...].astype(f32)
    gate = jnp.where(info_ref[0] == 1, sea, jnp.ones_like(sea))
    coup = gate * coup_ref[...]
    nat_ref[0:16] = gate * diff_ref[...]
    nat_ref[16:32] = gate
    nat_ref[32:48] = coup
    nat_ref[48:64] = coup * sea
    copies[3].wait()
    for f in range(2):
        nat_ref[64 * (f + 1) : 64 * (f + 2)] = state_ref[f * LEV * CX : f * LEV * CX + 64]
    for k in range(NAT):
        at = k * NEAR
        side_ref[at : at + NEAR] = nat_ref[k * CX : k * CX + NEAR]
        side_ref[SIDE_NAT + at : SIDE_NAT + at + NEAR] = nat_ref[(k + 1) * CX - NEAR : (k + 1) * CX]
    for x in range(CX):
        row = state_ref[pl.ds(x, LANES, stride=CX), :].T
        cells_ref[x] = row
        at = SIDE + 2 * HALO * x
        side_ref[at : at + HALO] = row[0:HALO]
        side_ref[at + HALO : at + 2 * HALO] = row[LANES - HALO :]


def prepare(info, state, diffusion, coupling, land_sea):
    tile = pltpu.VMEM((CX, LANES), f32)
    return pl.pallas_call(
        prepare_kernel,
        in_specs=[SM] + [HB] * 4,
        out_specs=[VM] * 3,
        out_shape=[
            struct(CX, LANES, LANES), struct(NAT * CX, LANES), struct(SIDE_ROWS, LANES),
        ],
        scratch_shapes=[
            pltpu.VMEM(state.shape, f32), tile, tile, pltpu.VMEM((CX, LANES), jnp.int32),
            pltpu.SemaphoreType.DMA((4,)),
        ],
        compiler_params=params(),
        name="prepare",
    )(info, *in_hbm(state, diffusion, coupling, land_sea))


def pack_kernel(cells_ref, nat_ref, side_ref, low_ref, high_ref):
    for j in range(HALO):
        low_ref[j * LANES : (j + 1) * LANES] = cells_ref[j]
        high_ref[j * LANES : (j + 1) * LANES] = cells_ref[CX - HALO + j]
    for k in range(NAT):
        at = EDGE + k * NEAR
        low_ref[at : at + NEAR] = nat_ref[k * CX : k * CX + NEAR]
        high_ref[at : at + NEAR] = nat_ref[(k + 1) * CX - NEAR : (k + 1) * CX]
    low_ref[EDGE_NAT:] = side_ref[0:CORNER]
    high_ref[EDGE_NAT:] = side_ref[SIDE_ROWS - CORNER :]


def pack(cells, nat, side):
    return pl.pallas_call(
        pack_kernel,
        in_specs=[VM] * 3,
        out_specs=[VM] * 2,
        out_shape=[struct(EDGE_ROWS, LANES)] * 2,
        compiler_params=params(),
        name="pack",
    )(cells, nat, side)


def linear_step(planes, made, mixing, diff, gate, damp):
    out = []
    for k in range(made):
        c = planes[k] if k < len(planes) else None
        vert = None

        def add(total, term):
            return term if total is None else total + term

        m = mixing[k]
        if k + 1 < len(planes):
            vert = add(vert, m * planes[k + 1])
        if k > 0:
            vert = add(vert, m * planes[k - 1])
        if c is None:
            out.append(gate * vert)
            continue
        vert = add(vert, -(m if k == 0 else 2.0 * m) * c)
        lap = (
            pltpu.roll(c, 1, 0) + pltpu.roll(c, TALL - 1, 0)
            + pltpu.roll(c, 1, 1) + pltpu.roll(c, RING - 1, 1) - 4.0 * c
        )
        new = c + (diff * lap + gate * vert)
        out.append(new - damp * c if k == 0 else new)
    return out


def coefs(coef_ref):
    return [coef_ref[k * TALL : (k + 1) * TALL] for k in range(4)]


def gather_kernel(mix_ref, nat_ref, low_ref, high_ref, side_ref, coef_ref, top_ref):
    def plane(k):
        def part(ref, base):
            return ref[base + k * NEAR : base + (k + 1) * NEAR]

        own = [part(high_ref, EDGE), nat_ref[k * CX : (k + 1) * CX], part(low_ref, EDGE)]
        other = [
            part(high_ref, EDGE_NAT + HALO * 2 * HALO), part(side_ref, 0), part(side_ref, SIDE_NAT),
            part(low_ref, EDGE_NAT),
        ]
        return jnp.concatenate(
            [jnp.concatenate(own, axis=0), jnp.concatenate(other, axis=0)], axis=1
        )

    for k in range(4):
        coef_ref[k * TALL : (k + 1) * TALL] = plane(k)
    diff, gate, damp, _ = coefs(coef_ref)
    mixing = [mix_ref[k] for k in range(4)]
    for f in range(2):
        planes = [plane(4 + 4 * f + k) for k in range(4)]
        for made in (3, 2, 1):
            planes = linear_step(planes, made, mixing, diff, gate, damp)
        top_ref[f] = planes[0][NEAR : NEAR + CX, 0:LANES]


def gather(mixing, nat, halo):
    return pl.pallas_call(
        gather_kernel,
        in_specs=[SM] + [VM] * 4,
        out_specs=[VM] * 2,
        out_shape=[struct(4 * TALL, RING), struct(2, CX, LANES)],
        compiler_params=params(),
        name="gather",
    )(mixing, nat, *halo)


def forcing(info_ref, hops, coef_ref, work):
    own, low, high = hops
    work[0 : 4 * NEAR] = low[...]
    work[4 * NEAR : 4 * (NEAR + CX)] = own[...]
    work[4 * (NEAR + CX) : 4 * TALL] = high[...]
    north = info_ref[1] == 1
    scale = coef_ref[3 * TALL : 4 * TALL]
    out = []
    for f in range(2):
        one = work[pl.ds(f, TALL, stride=4), :]
        two = work[pl.ds(2 + f, TALL, stride=4), :]
        own = jnp.where(north, two, one)
        other = jnp.where(north, one, two)
        out.append(scale * jnp.concatenate([own, other], axis=1))
    return out


def response(force, mixing, diff, gate, damp):
    planes = [force]
    for made in (2, 3):
        planes = linear_step(planes, made, mixing, diff, gate, damp)
        planes[0] = planes[0] + force
    return planes


def turn_kernel(*refs):
    info_ref, mix_ref, coef_ref, top_ref = refs[:4]
    hops, routes_hbm, w_hbm = refs[4:7], refs[7:11], refs[11]
    send_ref, resp_ref = refs[12:14]
    routes, (w, surf, count, sems, work) = refs[14:18], refs[18:]
    fetch_start(routes_hbm, routes, w_hbm, w, sems)
    send_ref[...] = jnp.zeros_like(send_ref)
    diff, gate, damp, _ = coefs(coef_ref)
    mixing = [mix_ref[k] for k in range(3)]
    force = forcing(info_ref, hops, coef_ref, work)
    for f in range(2):
        planes = response(force[f], mixing, diff, gate, damp)
        top = top_ref[f] + planes[0][NEAR : NEAR + CX, 0:LANES]
        surf[pl.ds(f, CX, stride=8), :] = rounded(top)
        for k in range(3):
            resp_ref[3 * f + k] = planes[k]

    def put(group, row, out):
        send_ref[pl.ds(group * 8 + row, 1), :] = out[0:1]
        send_ref[pl.ds(group * 8 + row + 1, 1), :] = out[1:2]

    write_contributions(routes_hbm, routes, w_hbm, w, sems, surf, count, put, None)


def turn(info, mixing, coef, top, hops, routes, weights, columns):
    pairs = weights.shape[0]
    return pl.pallas_call(
        turn_kernel,
        in_specs=[SM, SM] + [VM] * 5 + [HB] * 5,
        out_specs=[VM] * 2,
        out_shape=[struct(columns * 8, LANES), struct(6, TALL, RING)],
        scratch_shapes=pair_scratch(pairs, columns) + [pltpu.VMEM((4 * TALL, LANES), f32)],
        compiler_params=params(),
        name="turn",
    )(info, mixing, coef, top, *hops, *in_hbm(*routes, weights))


def sum_blocks(got_ref, chunk, marks, dense_ref):
    columns = got_ref.shape[0] // chunk
    for part in range(2):
        total = None
        for slot in range(2):
            k = part * 4 + slot * 2
            vals = [got_ref[pl.ds(k + f, columns, stride=chunk), :] for f in range(2)]
            vals = jnp.concatenate(vals, axis=1)
            vals = jnp.concatenate([vals, jnp.zeros((LANES - columns, RING), f32)], axis=0)
            seg = (part * 2 + slot) * CX
            here = exact_dot(marks[seg : seg + CX], vals)
            total = here if total is None else total + here
        for f in range(2):
            dense_ref[pl.ds(part * 2 + f, CX, stride=4), :] = total[:, f * LANES : (f + 1) * LANES]


def first_dense_kernel(got_ref, dense_ref, marks_ref):
    columns = got_ref.shape[0] // 9
    marks = got_ref[pl.ds(8, columns, stride=9), :]
    marks = jnp.concatenate([marks, jnp.zeros((LANES - columns, LANES), f32)], axis=0).T
    marks_ref[...] = marks[0:64]
    sum_blocks(got_ref, 9, marks, dense_ref)


def next_dense_kernel(got_ref, marks_ref, dense_ref):
    sum_blocks(got_ref, 8, marks_ref[...], dense_ref)


def densify(got, marks):
    first = marks is None
    out = struct(64, LANES)
    return pl.pallas_call(
        first_dense_kernel if first else next_dense_kernel,
        in_specs=[VM] if first else [VM, VM],
        out_specs=[VM, VM] if first else VM,
        out_shape=[out, out] if first else out,
        compiler_params=params(),
        name="densify",
    )(*([got] if first else [got, marks]))


def widen(own, other):
    return jnp.concatenate([other[120:128], own, other[0:8]], axis=0)


def bulk_kernel(
    mixrow_ref, mix_ref, cells_ref, coef_ref, resp_ref,
    low_ref, high_ref, side_ref,
    out_ref, top_ref, fa, fb, diff, gate, self_, work,
):
    lanes = lax.broadcasted_iota(jnp.int32, (1, LANES), 1)
    level = jnp.where(lanes >= LEV, lanes - LEV, lanes)
    mix = mixrow_ref[...]
    mix_up = jnp.where(level == LEV - 1, 0.0, mix)
    mix_low = jnp.where(level == 0, 0.0, mix)
    mix_mid = -(mix_up + mix_low)

    for x in range(CX):
        at = SIDE + 2 * HALO * x
        fa[HALO + x, 16:144] = cells_ref[x]
        fa[HALO + x, 16 - HALO : 16] = side_ref[at + HALO : at + 2 * HALO]
        fa[HALO + x, 144 : 144 + HALO] = side_ref[at : at + HALO]
    for j in range(HALO):
        for x, along, base in ((j, high_ref, EDGE_NAT), (HALO + CX + j, low_ref, EDGE_NAT + NAT * NEAR)):
            at = base + 2 * HALO * j
            fa[x, 16:144] = along[j * LANES : (j + 1) * LANES]
            fa[x, 16 - HALO : 16] = along[at + HALO : at + 2 * HALO]
            fa[x, 144 : 144 + HALO] = along[at : at + HALO]

    work[...] = jnp.zeros_like(work)

    def columns_of(one, two):
        wide = []
        for part in range(2):
            at = slice(part * LANES, (part + 1) * LANES)
            work[0:TALL] = coef_ref[one * TALL : (one + 1) * TALL, at]
            work[64 : 64 + TALL] = coef_ref[two * TALL : (two + 1) * TALL, at]
            wide.append(work[...].T)
        return widen(*wide)

    both = columns_of(0, 1)
    damping = columns_of(2, 2)
    for i in range(CX + 2 * HALO - 2):
        at = i + NEAR - HALO + 1
        d = jnp.broadcast_to(both[:, at : at + 1], (WIDE, LANES))
        g = jnp.broadcast_to(both[:, 64 + at : 65 + at], (WIDE, LANES))
        damp = jnp.where(level == 0, pltpu.roll(damping, LANES - at, 1), 0.0)
        diff[i] = d
        gate[i] = g
        self_[i] = (1.0 - 4.0 * d) + (g * mix_mid - damp)

    def advance(src, dst, x):
        for y in range(8, 8 + WIDE, CHUNK):
            at = slice(y, y + CHUNK)
            k = slice(y - 8, y - 8 + CHUNK)
            c = src[x, at]
            near = (src[x - 1, at] + src[x + 1, at]) + (
                src[x, y - 1 : y - 1 + CHUNK] + src[x, y + 1 : y + 1 + CHUNK]
            )
            vert = mix_up * pltpu.roll(c, LANES - 1, 1) + mix_low * pltpu.roll(c, 1, 1)
            dst[x, at] = self_[x - 1, k] * c + diff[x - 1, k] * near + gate[x - 1, k] * vert

    src, dst = fa, fb
    for step in range(1, HALO + 1):

        def body(x, carry, src=src, dst=dst):
            advance(src, dst, x)
            return carry

        lax.fori_loop(step, CX + 2 * HALO - step, body, 0, unroll=True)
        src, dst = dst, src
    for x in range(CX):
        out_ref[pl.ds(x, LANES, stride=CX), :] = src[HALO + x, 16:144].T

    d, g, c, _ = coefs(coef_ref)
    mixing = [mix_ref[k] for k in range(6)]
    for f in range(2):
        planes = [resp_ref[3 * f + k] for k in range(3)]
        for made in (4, 5, 6):
            planes = linear_step(planes, made, mixing, d, g, c)
        for k in range(6):
            at = (f * LEV + k) * CX
            full = out_ref[at : at + CX] + planes[k][NEAR : NEAR + CX, 0:LANES]
            out_ref[at : at + CX] = full
            if k < 3:
                top_ref[f, k] = full


def bulk(mixrow, mixing, cells, coef, resp, halo):
    big = pltpu.VMEM((CX + 2 * HALO, WIDE + 16, LANES), f32)
    coefficient = pltpu.VMEM((CX + 2 * HALO - 2, WIDE, LANES), f32)
    return pl.pallas_call(
        bulk_kernel,
        in_specs=[VM, SM] + [VM] * 6,
        out_specs=[VM, VM],
        out_shape=[struct(2 * LEV * CX, LANES), struct(2, 3, CX, LANES)],
        scratch_shapes=[big, big] + [coefficient] * 3 + [pltpu.VMEM((LANES, LANES), f32)],
        compiler_params=params(),
        cost_estimate=pl.CostEstimate(flops=40_000_000, transcendentals=0, bytes_accessed=40_000_000),
        name="bulk",
    )(mixrow, mixing, cells, coef, resp, *halo)


def final_kernel(info_ref, mix_ref, coef_ref, own, low, high, top_ref, part_ref, out_ref, work):
    diff, gate, damp, _ = coefs(coef_ref)
    mixing = [mix_ref[k] for k in range(3)]
    force = forcing(info_ref, (own, low, high), coef_ref, work)
    for f in range(2):
        planes = response(force[f], mixing, diff, gate, damp)
        for k in range(3):
            out_ref[f, k] = top_ref[f, k] + planes[k][NEAR : NEAR + CX, 0:LANES]


def final(info, mixing, coef, hops, top, part):
    block = pl.BlockSpec((2, 3, CX, LANES), lambda i: (0, 0, 0, 0))
    return pl.pallas_call(
        final_kernel,
        grid=(1,),
        in_specs=[SM, SM] + [VM] * 5 + [HB],
        out_specs=block,
        out_shape=struct(2, LEV, CX, LANES),
        input_output_aliases={7: 0},
        scratch_shapes=[pltpu.VMEM((4 * TALL, LANES), f32)],
        compiler_params=params(),
        name="final",
    )(info, mixing, coef, *hops, top, part)


def solution(mesh):
    comps, columns, halves = (mesh.shape[a] for a in AXES)

    def sent(value, where):
        pairs = []
        for s in range(comps):
            for g in range(columns):
                for h in range(halves):
                    a, b, c = where(s, g, h)
                    b, c = b % columns, c % halves
                    pairs.append(((s * columns + g) * halves + h, (a * columns + b) * halves + c))
        return lax.ppermute(value, AXES, pairs)

    def hopped(dense):
        full = dense + sent(dense, lambda s, g, h: (s, g, h + 1))
        return (
            sent(full, lambda s, g, h: (1 - s, g, h)),
            sent(full[4 * (CX - NEAR) :], lambda s, g, h: (1 - s, g + 1, h)),
            sent(full[: 4 * NEAR], lambda s, g, h: (1 - s, g - 1, h)),
        )

    def body(
        state, diffusion, vertical, coupling, land_sea,
        route_tile, route_src, route_dst, pair_cols, intersection,
    ):
        info = jnp.stack([lax.axis_index("comp"), lax.axis_index("gy")]).astype(jnp.int32)
        mixing = vertical[0]
        mixrow = jnp.concatenate([vertical, vertical], axis=1)
        routes = (route_tile[0, 0, :, 0], route_src[0, 0], route_dst[0, 0], pair_cols[0, 0])
        weights = intersection[0, 0]

        cells, nat, side = prepare(
            info, state.reshape(-1, LANES), diffusion[0], coupling[0], land_sea[0]
        )
        side = sent(side, lambda s, g, h: (s, g, h + 1))
        send = first_contributions(routes, weights, state[0], columns)
        send, side = lax.optimization_barrier((send, side))
        got = lax.all_to_all(send, "gx", 0, 0, tiled=True)
        low, high = pack(cells, nat, side)
        halo = (
            sent(low, lambda s, g, h: (s, g - 1, h)),
            sent(high, lambda s, g, h: (s, g + 1, h)),
            side,
        )
        coef, top = gather(mixing, nat, halo)
        dense, marks = densify(got.reshape(-1, LANES), None)
        hops = hopped(dense)
        send, resp = turn(info, mixing, coef, top, hops, routes, weights, columns)

        got = lax.all_to_all(send, "gx", 0, 0, tiled=True)
        part, low = bulk(mixrow, mixing, cells, coef, resp, halo)
        got, part, low = lax.optimization_barrier((got, part, low))
        hops = hopped(densify(got, marks))
        out = final(info, mixing, coef, hops, low, part.reshape(state.shape[1:]))
        return out[None]

    spec = P("comp", "gx", "gy")
    route = P("comp", ("gx", "gy"))
    return jax.shard_map(
        body,
        mesh=mesh,
        in_specs=(
            P("comp", None, None, "gx", "gy"), spec, P("comp", None), spec, spec,
            route, route, route, route, route,
        ),
        out_specs=P("comp", None, None, "gx", "gy"),
        check_vma=False,
    )
```
